128 devices in a mesh: lon: 32 (over z, x, y_hi), lat: 4 (over y_lo, core).
Axes of the slice: x: 4, y: 4 (y_hi: 2, y_lo: 2; y = y_hi * 2 + y_lo), z: 4, core: 2. Of those that a mesh axis runs over, the one named last changes fastest.
Arguments:
- ocean_state: float32 [4, 3, 512, 8192], P(None, None, 'lat', 'lon'), may hold values from -6 to 6
- mixing: float32 [3, 512, 8192], P(None, 'lat', 'lon'), may hold values from 0.1 to 1
- land_sea: int32 [512, 8192], P('lat', 'lon'), may hold values 0 or 1
Outputs:
- final_state: float32 [4, 3, 512, 8192], P(None, None, 'lat', 'lon')
The draws below stay inside these ranges and needn't reach their ends.
All inputs are finite; a program needn't handle non-finite values. No bound on the sum of `land_sea` on one device may be relied on, other than what follows from the above.
Results may differ from the reference program's by a relative error of at most 0.000029.
Values sent between devices are 32-bit elements; how exact they have to be, the bound alone decides.
No kernel may reach another device: no remote copies, remote signals or barrier semaphores. Data moves between devices by JAX's collectives and lax.ppermute only.
A program may use at most 128 MiB of HBM per device.

```python
import math
import jax
import jax.numpy as jnp
from jax import lax

K = 3
STEPS = 8
NLAT = 512
NLON = 8192


def place_ends(values, own_key, smallest, high):
    shape = values.shape
    index_at = [jax.random.randint(jax.random.fold_in(own_key, axis), (), 0, shape[axis]) for axis in range(len(shape))]
    values = values.at[tuple(index_at)].set(smallest)
    longest = shape.index(max(shape))
    index_at[longest] = (index_at[longest] + 1) % shape[longest]
    return values.at[tuple(index_at)].set(high)


def shard_levels(rng, dims, pieces, least, high):
    loudness, own = 1.0, jax.random.fold_in(rng, 6)
    for dim, parts in pieces:
        steps = jnp.exp(jax.random.uniform(jax.random.fold_in(own, dim), (parts,), jnp.float32, least / len(pieces), high / len(pieces)))
        loudness = loudness * jnp.repeat(steps, dims[dim] // parts).reshape([-1 if axis == dim else 1 for axis in range(len(dims))])
    return loudness


def noise(key, dims, spread, bound, split=(), dtype=jnp.bfloat16):
    values = jax.random.normal(key, dims, jnp.float32) * spread
    if len(split) > 0:
        values = shard_levels(key, dims, split, -0.22, 0.18) * values
    return jnp.clip(values, min=-bound, max=bound).astype(dtype)


def setup_inputs(seed: int = 0) -> dict:
    arg_keys = jax.random.split(jax.random.key(seed), 4)
    return {
        "ocean_state": noise(arg_keys[0], (4, K, NLAT, NLON), 1.0, 6.0, ((2, 4), (3, 32)), jnp.float32),
        "mixing": jnp.clip(jnp.exp(math.log(1.0) - 2.3025851 * jax.random.uniform(arg_keys[1], (K, NLAT, NLON), jnp.float32) ** shard_levels(arg_keys[1], (K, NLAT, NLON), ((1, 4), (2, 32)), -0.2, 0.2)), 0.1, 1.0),
        "land_sea": place_ends((jax.random.randint(arg_keys[2], (NLAT, NLON), 0, 4) < 3).astype(jnp.int32), jax.random.fold_in(arg_keys[2], 1), 0, 1),
    }


THERMAL = 0.2
HALINE = 0.15
GRAVITY = 0.5
TIMESTEP = 0.1


def interior(padded, first_cut, last_cut, along):
    return lax.slice_in_dim(padded, first_cut, padded.shape[along] - last_cut, axis=along)


def flux_divergence(padded, along):
    speed_index = 2 if along == 3 else 3
    speeds = padded[speed_index:speed_index + 1]
    face_value = (7.0 * (interior(padded, 1, 2, along) + interior(padded, 2, 1, along)) - (interior(padded, 0, 3, along) + interior(padded, 3, 0, along))) / 12.0
    face_speed = 0.5 * (interior(speeds, 1, 2, along) + interior(speeds, 2, 1, along))
    face_flux = face_speed * face_value
    return interior(face_flux, 1, 0, along) - interior(face_flux, 0, 1, along)


def neighbours(padded, along):
    return interior(padded, 3, 1, along) + interior(padded, 1, 3, along)


def gradient(padded, along):
    return 0.5 * (interior(padded, 3, 1, along) - interior(padded, 1, 3, along))


def pressure(padded):
    density = -THERMAL * padded[0] + HALINE * padded[1]
    return jnp.cumsum(density, axis=0)


def advance(center, lon_padded, lat_padded, mixing, coriolis, wetness):
    advection = flux_divergence(lon_padded, 3) + flux_divergence(lat_padded, 2)
    laplacian = neighbours(lon_padded, 3) + neighbours(lat_padded, 2) - 4.0 * center
    grad_lon = gradient(pressure(lon_padded), 2)
    grad_lat = gradient(pressure(lat_padded), 1)
    tracers = center[:2]
    upper_level = jnp.concatenate([tracers[:, :1], tracers[:, :-1]], axis=1)
    lower_level = jnp.concatenate([tracers[:, 1:], tracers[:, -1:]], axis=1)
    vertical = upper_level + lower_level - 2.0 * tracers
    tracer_tend = -advection[:2] + mixing * laplacian[:2] + 0.5 * mixing * vertical
    zonal_tend = -advection[2] + coriolis * center[3] - GRAVITY * grad_lon + mixing * laplacian[2]
    merid_tend = -advection[3] - coriolis * center[2] - GRAVITY * grad_lat + mixing * laplacian[3]
    tendency = jnp.concatenate([tracer_tend, zonal_tend[None], merid_tend[None]], axis=0)
    return center + TIMESTEP * wetness * tendency


def reference(ocean_state, mixing, land_sea):
    wetness = land_sea.astype(jnp.float32)
    row_index = jnp.arange(NLAT).astype(jnp.float32)
    coriolis = jnp.sin(jnp.pi * (row_index + 0.5) / NLAT - jnp.pi / 2)[:, None]
    parity = jnp.array([1.0, 1.0, -1.0, -1.0], jnp.float32).reshape(4, 1, 1, 1)
    current = ocean_state
    for substep in range(STEPS):
        lon_padded = jnp.concatenate([current[..., -2:], current, current[..., :2]], axis=3)
        ghost_rows = current[:, :, NLAT - 2:, ::-1][:, :, ::-1, :] * parity
        south_rows = jnp.zeros_like(current[:, :, :2, :])
        lat_padded = jnp.concatenate([south_rows, current, ghost_rows], axis=2)
        current = advance(current, lon_padded, lat_padded, mixing, coriolis, wetness)
    return current
```

```python
import functools
import jax
import jax.numpy as jnp
from jax import lax
from jax.experimental import pallas as pl
from jax.experimental.pallas import tpu as pltpu
from jax.sharding import PartitionSpec as P

STEPS = 8
K = 3
HALO = 2 * STEPS
LANES = 128
PAD = 8

THERMAL = 0.2
HALINE = 0.15
GRAVITY = 0.5
TIMESTEP = 0.1

STATE = 4 * K
PLANES = STATE + K + 1
VMEM_LIMIT = 48 * 1024 * 1024
SPANS = (21, 19, 19, 19, 19, 17, 17, 17)


def params():
    return pltpu.CompilerParams(vmem_limit_bytes=VMEM_LIMIT)


def shifted(x, by):
    return pltpu.roll(x, by % LANES, 1)


def pack_rows_kernel(xl, xh, ml, mh, wl, wh, to_a, to_b):
    even = lax.rem(lax.axis_index("lat"), 2) == 0

    def fill(dest, x, m, w):
        dest[:STATE] = x[...]
        dest[STATE : STATE + K] = m[...]
        dest[STATE + K] = TIMESTEP * w[...].astype(jnp.float32)

    @pl.when(even)
    def _():
        fill(to_b, xh, mh, wh)
        fill(to_a, xl, ml, wl)

    @pl.when(jnp.logical_not(even))
    def _():
        fill(to_b, xl, ml, wl)
        fill(to_a, xh, mh, wh)


def pack_rows(x, mixing, land):
    rows, cols = land.shape
    last = rows // HALO - 1
    specs = []
    for lead in ((STATE,), (K,), ()):
        for at in (0, last):
            specs.append(pl.BlockSpec(lead + (HALO, cols), functools.partial(lambda at, n, g: (0,) * n + (at, 0), at, len(lead))))
    slab = jax.ShapeDtypeStruct((PLANES, HALO, cols), jnp.float32)
    return pl.pallas_call(
        pack_rows_kernel,
        grid=(1,),
        in_specs=specs,
        out_specs=[pl.BlockSpec(slab.shape, lambda g: (0, 0, 0))] * 2,
        out_shape=[slab, slab],
        compiler_params=params(),
        name="pack_rows",
    )(x, x, mixing, mixing, land, land)


def fold(slab):
    planes, rows, cols = slab.shape
    flat = slab.reshape(planes * rows, cols)
    n = planes * rows
    i = lax.broadcasted_iota(jnp.int32, (n, n), 0)
    j = lax.broadcasted_iota(jnp.int32, (n, n), 1)
    plane = i // rows
    sign = jnp.where(jnp.logical_and(plane >= 2 * K, plane < STATE), -1.0, 1.0)
    left = jnp.where(j == plane * rows + (rows - 1 - (i - plane * rows)), sign, 0.0).astype(jnp.float32)
    a = lax.broadcasted_iota(jnp.int32, (cols, cols), 0)
    b = lax.broadcasted_iota(jnp.int32, (cols, cols), 1)
    right = jnp.where(a + b == cols - 1, 1.0, 0.0).astype(jnp.float32)
    dot = functools.partial(jnp.dot, precision=lax.Precision.HIGHEST, preferred_element_type=jnp.float32)
    return dot(dot(left, flat), right).reshape(slab.shape)


def extend_kernel(x, m, w, ra, rb, tiles, send_low, send_high, cor, south, north):
    lat = lax.axis_index("lat")
    even = lax.rem(lat, 2) == 0
    block = x.shape[1]
    total = block * lax.axis_size("lat")

    @pl.when(even)
    def _():
        north[...] = rb[...]
        south[...] = ra[...]

    @pl.when(jnp.logical_not(even))
    def _():
        south[...] = rb[...]

        @pl.when(lat == lax.axis_size("lat") - 1)
        def _():
            north[...] = fold(ra[...])

        @pl.when(lat != lax.axis_size("lat") - 1)
        def _():
            north[...] = ra[...]

    row = lax.broadcasted_iota(jnp.int32, cor.shape, 0) + (lat * block - HALO - PAD)
    cor[...] = jnp.sin(jnp.pi * (row.astype(jnp.float32) + 0.5) / total - jnp.pi / 2)

    def put(at, planes, low, high, rows):
        lane = lax.broadcasted_iota(jnp.int32, (rows, LANES), 1)
        packs = []
        for p, lo, hi in zip(planes, low, high):
            here = pl.ds(at, rows)
            tiles[0, p, here] = lo
            tiles[1, p, here] = jnp.where(lane < 32, shifted(lo, -96), shifted(hi, 32))
            edge = jnp.where(lane < 48, shifted(lo, 16), shifted(hi, -16))
            tiles[2, p, here] = edge
            packs.append((lo, hi))
        return packs

    def rows_at(at, source, rows):
        lane = lax.broadcasted_iota(jnp.int32, (rows, LANES), 1)
        for group in range(PLANES // 8):
            low = jnp.zeros((rows, LANES), jnp.float32)
            high = jnp.zeros((rows, LANES), jnp.float32)
            for q in range(8):
                p = group * 8 + q
                lo, hi = source(p)
                put(PAD + at, [p], [lo], [hi], rows)
                mine = jnp.logical_and(lane >= 16 * q, lane < 16 * q + 16)
                low = jnp.where(mine, shifted(lo, 16 * q), low)
                high = jnp.where(mine, shifted(hi, 16 * q - 112), high)
            send_low[group, pl.ds(at, rows)] = low
            send_high[group, pl.ds(at, rows)] = high

    def from_slab(ref, r):
        def source(p):
            return ref[p, pl.ds(r, 8), :LANES], ref[p, pl.ds(r, 8), LANES:]
        return source

    for r in range(0, HALO, 8):
        rows_at(r, from_slab(south, r), 8)
        rows_at(HALO + block + r, from_slab(north, r), 8)

    @pl.loop(0, block // 8)
    def _(g):
        r = pl.multiple_of(g * 8, 8)

        def source(p):
            if p < STATE:
                return x[p, pl.ds(r, 8), :LANES], x[p, pl.ds(r, 8), LANES:]
            if p < STATE + K:
                return m[p - STATE, pl.ds(r, 8), :LANES], m[p - STATE, pl.ds(r, 8), LANES:]
            return (
                TIMESTEP * w[pl.ds(r, 8), :LANES].astype(jnp.float32),
                TIMESTEP * w[pl.ds(r, 8), LANES:].astype(jnp.float32),
            )

        rows_at(HALO + r, source, 8)


def extend(x, mixing, land, ra, rb):
    block, cols = land.shape
    span = block + 2 * HALO
    f32 = jnp.float32
    vmem = pl.BlockSpec(memory_space=pltpu.VMEM)
    return pl.pallas_call(
        extend_kernel,
        in_specs=[vmem] * 5,
        out_specs=[vmem] * 4,
        out_shape=[
            jax.ShapeDtypeStruct((3, PLANES, span + 2 * PAD, LANES), f32),
            jax.ShapeDtypeStruct((PLANES // 8, span, LANES), f32),
            jax.ShapeDtypeStruct((PLANES // 8, span, LANES), f32),
            jax.ShapeDtypeStruct((span + 2 * PAD, LANES), f32),
        ],
        scratch_shapes=[pltpu.VMEM((PLANES, HALO, cols), f32)] * 2,
        compiler_params=params(),
        name="extend",
    )(x, mixing, land, ra, rb)


def substep(src, dst, coef, cor, start, dst_start, span, unroll=1):
    def load(ref, p, t):
        return ref[p, pl.ds(start + t, 8, stride=span), :]

    def face(prev, here, nxt, nxt2):
        a = here + nxt
        return a, 7.0 * a - (prev + nxt2)

    def density(t, k):
        return -0.25 * THERMAL * load(src, k, t) + 0.25 * HALINE * load(src, K + k, t)

    def pressures(t):
        out = [density(t, 0)]
        for k in range(1, K):
            out.append(out[-1] + density(t, k))
        return out

    def fluxes(t):
        out = [None] * STATE
        for k in range(K):
            order = [3, 0, 1, 2]
            speed = None
            for f in order:
                p = f * K + k
                a, value = face(load(src, p, t - 1), load(src, p, t), load(src, p, t + 1), load(src, p, t + 2))
                if f == 3:
                    speed = a
                out[p] = speed * value
        return out

    def row(t, carry):
        below_flux, p_prev, p_here = carry
        wet = coef(15)(t)
        wet24 = wet * (1.0 / 24.0)
        wet_cor = wet * cor[pl.ds(start + t, 8, stride=span), :]
        p_next = pressures(t + 1)
        above = fluxes(t)
        for k in range(K):
            wet_mix = wet * coef(STATE + k)(t)
            speed = None
            for f in (2, 3, 0, 1):
                p = f * K + k
                q = load(src, p, t)
                east = shifted(q, -1)
                west = shifted(q, 1)
                a, value = face(west, q, east, shifted(q, -2))
                if f == 2:
                    speed = a
                flux = speed * value
                adv = (flux - shifted(flux, 1)) + (above[p] - below_flux[p])
                lap = (east + west) + (load(src, p, t + 1) + load(src, p, t - 1))
                if f < 2:
                    if 0 < k < K - 1:
                        lap = lap + 0.5 * (load(src, p - 1, t) + load(src, p + 1, t)) - 5.0 * q
                    elif k == 0:
                        lap = lap + 0.5 * load(src, p + 1, t) - 4.5 * q
                    else:
                        lap = lap + 0.5 * load(src, p - 1, t) - 4.5 * q
                else:
                    lap = lap - 4.0 * q
                new = q + (wet_mix * lap - wet24 * adv)
                if f == 2:
                    grad = shifted(p_here[k], -1) - shifted(p_here[k], 1)
                    new = new + (wet_cor * load(src, p + K, t) - wet * grad)
                if f == 3:
                    grad = p_next[k] - p_prev[k]
                    new = new - (wet_cor * load(src, p - K, t) + wet * grad)
                dst[p, pl.ds(dst_start + t, 8, stride=span), :] = new
        return above, p_here, p_next

    init = (fluxes(-1), pressures(-1), pressures(0))
    lax.fori_loop(0, span, row, init, unroll=unroll)


def window(tile, cor, even, odd, out):
    span_rows = tile.shape[1] - 2 * PAD
    src = tile
    for s in range(STEPS):
        span = SPANS[s]
        need = span_rows - 4 * (s + 1)
        spare = (8 * span - need) // 2
        start = PAD + 2 * (s + 1) - spare
        dst = out if s == STEPS - 1 else (even if s % 2 == 0 else odd)
        dst_start = PAD - spare if s == STEPS - 1 else start

        def coef(p, start=start, span=span):
            return lambda t: tile[p, pl.ds(start + t, 8, stride=span), :]

        substep(src, dst, coef, cor, start, dst_start, span)
        src = dst


def interior_kernel(tiles, cor, out, even, odd):
    @pl.loop(0, 2)
    def _(i):
        window(tiles.at[i], cor, even, odd, out.at[i])


def interior(tiles, cor):
    rows = tiles.shape[2]
    block = rows - 2 * PAD - 2 * HALO
    vmem = pl.BlockSpec(memory_space=pltpu.VMEM)
    cells = 2 * STATE * rows * LANES
    return pl.pallas_call(
        interior_kernel,
        in_specs=[pl.BlockSpec((2,) + tiles.shape[1:], lambda g: (0, 0, 0, 0)), pl.BlockSpec(cor.shape, lambda g: (0, 0))],
        out_specs=pl.BlockSpec((2, STATE, block + 2 * PAD, LANES), lambda g: (0, 0, 0, 0)),
        grid=(1,),
        out_shape=jax.ShapeDtypeStruct((2, STATE, block + 2 * PAD, LANES), jnp.float32),
        scratch_shapes=[pltpu.VMEM((STATE, rows, LANES), jnp.float32)] * 2,
        compiler_params=params(),
        cost_estimate=pl.CostEstimate(flops=STEPS * 30 * cells, transcendentals=0, bytes_accessed=8 * cells),
        name="interior",
    )(tiles, cor)


def edge_kernel(tiles, cor, got_low, got_high, inner, out, tile, even, odd, edge):
    span = got_low.shape[1]
    block = out.shape[1]

    @pl.loop(0, span // 8)
    def _(g):
        r = pl.multiple_of(g * 8, 8)
        lane = lax.broadcasted_iota(jnp.int32, (8, LANES), 1)
        for p in range(PLANES):
            left = shifted(got_low[p // 8, pl.ds(r, 8)], -16 * (p % 8))
            right = shifted(got_high[p // 8, pl.ds(r, 8)], 112 - 16 * (p % 8))
            mid = tiles[0, p, pl.ds(PAD + r, 8)]
            tile[p, pl.ds(PAD + r, 8)] = jnp.where(lane < 16, left, jnp.where(lane >= 112, right, mid))

    window(tile, cor, even, odd, edge)

    @pl.loop(0, block // 8)
    def _(g):
        r = pl.multiple_of(g * 8, 8)
        lane = lax.broadcasted_iota(jnp.int32, (8, LANES), 1)
        for p in range(STATE):
            here = pl.ds(PAD + r, 8)
            e = edge[p, here]
            lo = inner[0, p, here]
            hi = inner[1, p, here]
            out[p, pl.ds(r, 8), :LANES] = jnp.where(lane < 16, shifted(e, -16), jnp.where(lane < 112, lo, shifted(hi, 96)))
            out[p, pl.ds(r, 8), LANES:] = jnp.where(lane < 80, shifted(hi, -32), shifted(e, 16))


def edges(tiles, cor, got_low, got_high, inner, cols):
    rows = tiles.shape[2]
    block = rows - 2 * PAD - 2 * HALO
    whole = lambda a: pl.BlockSpec(a.shape, functools.partial(lambda n, g: (0,) * n, len(a.shape)))
    f32 = jnp.float32
    shape = jax.ShapeDtypeStruct((STATE, block, cols), f32)
    return pl.pallas_call(
        edge_kernel,
        grid=(1,),
        in_specs=[pl.BlockSpec((1,) + tiles.shape[1:], lambda g: (2, 0, 0, 0)), whole(cor), whole(got_low), whole(got_high), whole(inner)],
        out_specs=whole(shape),
        out_shape=shape,
        scratch_shapes=[
            pltpu.VMEM((PLANES, rows, LANES), f32),
            pltpu.VMEM((STATE, rows, LANES), f32),
            pltpu.VMEM((STATE, rows, LANES), f32),
            pltpu.VMEM((STATE, block + 2 * PAD, LANES), f32),
        ],
        compiler_params=params(),
        name="edges",
    )(tiles, cor, got_low, got_high, inner)


def body(ocean_state, mixing, land_sea):
    block, cols = land_sea.shape
    n_lon, n_lat = lax.axis_size("lon"), lax.axis_size("lat")
    axes = ("lon", "lat")

    def at(i, l):
        return (i % n_lon) * n_lat + l

    pairs_b = [(at(i, l), at(i, l ^ 1)) for i in range(n_lon) for l in range(n_lat)]
    pairs_a = []
    for i in range(n_lon):
        for l in range(1, n_lat - 1, 2):
            pairs_a += [(at(i, l), at(i, l + 1)), (at(i, l + 1), at(i, l))]
        pairs_a.append((at(i, n_lat - 1), at(n_lon - 1 - i, n_lat - 1)))
    east = [(i, (i + 1) % n_lon) for i in range(n_lon)]
    west = [((i + 1) % n_lon, i) for i in range(n_lon)]

    x = ocean_state.reshape(STATE, block, cols)
    to_a, to_b = pack_rows(x, mixing, land_sea)
    ra = lax.ppermute(to_a, axes, pairs_a)
    rb = lax.ppermute(to_b, axes, pairs_b)
    tiles, send_low, send_high, cor = extend(x, mixing, land_sea, ra, rb)
    got_low = lax.ppermute(send_high, "lon", east)
    got_high = lax.ppermute(send_low, "lon", west)
    inner = interior(tiles, cor)
    out = edges(tiles, cor, got_low, got_high, inner, cols)
    return out.reshape(ocean_state.shape)


def solution(mesh):
    in_specs = (P(None, None, "lat", "lon"), P(None, "lat", "lon"), P("lat", "lon"))
    out_specs = P(None, None, "lat", "lon")
    return jax.shard_map(body, mesh=mesh, in_specs=in_specs, out_specs=out_specs, check_vma=False)
```

```python
import functools
import jax
import jax.numpy as jnp
from jax import lax
from jax.experimental import pallas as pl
from jax.experimental.pallas import tpu as pltpu
from jax.sharding import PartitionSpec as P

STEPS = 8
K = 3
HALO = 2 * STEPS
LANES = 128
PAD = 8

THERMAL = 0.2
HALINE = 0.15
GRAVITY = 0.5
TIMESTEP = 0.1

STATE = 4 * K
PLANES = STATE + K + 1
VMEM_LIMIT = 48 * 1024 * 1024
SPANS = (21, 19, 19, 19, 19, 17, 17, 17)


def params():
    return pltpu.CompilerParams(vmem_limit_bytes=VMEM_LIMIT)


def shifted(x, by):
    return pltpu.roll(x, by % LANES, 1)


def pack_rows_kernel(xl, xh, ml, mh, wl, wh, to_a, to_b):
    even = lax.rem(lax.axis_index("lat"), 2) == 0

    def fill(dest, x, m, w):
        dest[:STATE] = x[...]
        dest[STATE : STATE + K] = m[...]
        dest[STATE + K] = TIMESTEP * w[...].astype(jnp.float32)

    @pl.when(even)
    def _():
        fill(to_b, xh, mh, wh)
        fill(to_a, xl, ml, wl)

    @pl.when(jnp.logical_not(even))
    def _():
        fill(to_b, xl, ml, wl)
        fill(to_a, xh, mh, wh)


def pack_rows(x, mixing, land):
    rows, cols = land.shape
    last = rows // HALO - 1
    specs = []
    for lead in ((STATE,), (K,), ()):
        for at in (0, last):
            specs.append(pl.BlockSpec(lead + (HALO, cols), functools.partial(lambda at, n, g: (0,) * n + (at, 0), at, len(lead))))
    slab = jax.ShapeDtypeStruct((PLANES, HALO, cols), jnp.float32)
    return pl.pallas_call(
        pack_rows_kernel,
        grid=(1,),
        in_specs=specs,
        out_specs=[pl.BlockSpec(slab.shape, lambda g: (0, 0, 0))] * 2,
        out_shape=[slab, slab],
        compiler_params=params(),
        name="pack_rows",
    )(x, x, mixing, mixing, land, land)


def fold(slab):
    planes, rows, cols = slab.shape
    flat = slab.reshape(planes * rows, cols)
    n = planes * rows
    i = lax.broadcasted_iota(jnp.int32, (n, n), 0)
    j = lax.broadcasted_iota(jnp.int32, (n, n), 1)
    plane = i // rows
    sign = jnp.where(jnp.logical_and(plane >= 2 * K, plane < STATE), -1.0, 1.0)
    left = jnp.where(j == plane * rows + (rows - 1 - (i - plane * rows)), sign, 0.0).astype(jnp.float32)
    a = lax.broadcasted_iota(jnp.int32, (cols, cols), 0)
    b = lax.broadcasted_iota(jnp.int32, (cols, cols), 1)
    right = jnp.where(a + b == cols - 1, 1.0, 0.0).astype(jnp.float32)
    dot = functools.partial(jnp.dot, precision=lax.Precision.HIGHEST, preferred_element_type=jnp.float32)
    return dot(dot(left, flat), right).reshape(slab.shape)


def extend_kernel(x, m, w, ra, rb, tiles, send_low, send_high, cor, south, north):
    lat = lax.axis_index("lat")
    even = lax.rem(lat, 2) == 0
    block = x.shape[1]
    total = block * lax.axis_size("lat")

    @pl.when(even)
    def _():
        north[...] = rb[...]
        south[...] = ra[...]

    @pl.when(jnp.logical_not(even))
    def _():
        south[...] = rb[...]

        @pl.when(lat == lax.axis_size("lat") - 1)
        def _():
            north[...] = fold(ra[...])

        @pl.when(lat != lax.axis_size("lat") - 1)
        def _():
            north[...] = ra[...]

    row = lax.broadcasted_iota(jnp.int32, cor.shape, 0) + (lat * block - HALO - PAD)
    cor[...] = jnp.sin(jnp.pi * (row.astype(jnp.float32) + 0.5) / total - jnp.pi / 2)

    def put(at, planes, low, high, rows):
        lane = lax.broadcasted_iota(jnp.int32, (rows, LANES), 1)
        packs = []
        for p, lo, hi in zip(planes, low, high):
            here = pl.ds(at, rows)
            tiles[0, p, here] = lo
            tiles[1, p, here] = jnp.where(lane < 96, hi, lo)
            tiles[2, p, here] = jnp.where(lane < 64, shifted(lo, 32), hi)
            packs.append((lo, hi))
        return packs

    def rows_at(at, source, rows):
        lane = lax.broadcasted_iota(jnp.int32, (rows, LANES), 1)
        for group in range(PLANES // 8):
            low = jnp.zeros((rows, LANES), jnp.float32)
            high = jnp.zeros((rows, LANES), jnp.float32)
            for q in range(8):
                p = group * 8 + q
                lo, hi = source(p)
                put(PAD + at, [p], [lo], [hi], rows)
                mine = jnp.logical_and(lane >= 16 * q, lane < 16 * q + 16)
                low = jnp.where(mine, shifted(lo, 16 * q), low)
                high = jnp.where(mine, shifted(hi, 16 * q - 112), high)
            send_low[group, pl.ds(at, rows)] = low
            send_high[group, pl.ds(at, rows)] = high

    def from_slab(ref, r):
        def source(p):
            return ref[p, pl.ds(r, 8), :LANES], ref[p, pl.ds(r, 8), LANES:]
        return source

    for r in range(0, HALO, 8):
        rows_at(r, from_slab(south, r), 8)
        rows_at(HALO + block + r, from_slab(north, r), 8)

    @pl.loop(0, block // 8)
    def _(g):
        r = pl.multiple_of(g * 8, 8)

        def source(p):
            if p < STATE:
                return x[p, pl.ds(r, 8), :LANES], x[p, pl.ds(r, 8), LANES:]
            if p < STATE + K:
                return m[p - STATE, pl.ds(r, 8), :LANES], m[p - STATE, pl.ds(r, 8), LANES:]
            return (
                TIMESTEP * w[pl.ds(r, 8), :LANES].astype(jnp.float32),
                TIMESTEP * w[pl.ds(r, 8), LANES:].astype(jnp.float32),
            )

        rows_at(HALO + r, source, 8)


def extend(x, mixing, land, ra, rb):
    block, cols = land.shape
    span = block + 2 * HALO
    f32 = jnp.float32
    vmem = pl.BlockSpec(memory_space=pltpu.VMEM)
    return pl.pallas_call(
        extend_kernel,
        in_specs=[vmem] * 5,
        out_specs=[vmem] * 4,
        out_shape=[
            jax.ShapeDtypeStruct((3, PLANES, span + 2 * PAD, LANES), f32),
            jax.ShapeDtypeStruct((PLANES // 8, span, LANES), f32),
            jax.ShapeDtypeStruct((PLANES // 8, span, LANES), f32),
            jax.ShapeDtypeStruct((span + 2 * PAD, LANES), f32),
        ],
        scratch_shapes=[pltpu.VMEM((PLANES, HALO, cols), f32)] * 2,
        compiler_params=params(),
        name="extend",
    )(x, mixing, land, ra, rb)


def line_weights():
    shape = (2 * LANES, LANES)
    here = lax.rem(lax.broadcasted_iota(jnp.int32, shape, 0), LANES)
    lane = lax.broadcasted_iota(jnp.int32, shape, 1)
    gap = lax.rem(here - lane + LANES, LANES)

    def stencil(terms):
        out = jnp.zeros(shape, jnp.float32)
        for offset, value in terms:
            out = jnp.where(gap == offset % LANES, value, out)
        return out

    east = stencil(((0, 7.0), (1, 7.0), (-1, -1.0), (2, -1.0)))
    west = stencil(((-1, 7.0), (0, 7.0), (-2, -1.0), (1, -1.0)))
    lap = stencil(((0, -4.0), (1, 1.0), (-1, 1.0)))
    diff = stencil(((1, 1.0), (-1, -1.0)))
    return jnp.concatenate([east, west, lap, diff], axis=1).astype(jnp.bfloat16)


def products(src, weights, prod, first, count):
    for f in range(4):
        planes = pl.ds(f * K, K)
        rows = pl.ds(first, count)
        q = src[planes, rows, :].reshape(K * count, LANES)
        high = q.astype(jnp.bfloat16)
        low = (q - high.astype(jnp.float32)).astype(jnp.bfloat16)
        both = jnp.concatenate([high, low], axis=1)
        got = jnp.dot(both, weights[...], preferred_element_type=jnp.float32)
        for j in range(4 if f < 3 else 3):
            prod[j, planes, rows, :] = got[:, j * LANES : (j + 1) * LANES].reshape(K, count, LANES)


def substep(src, dst, coef, cor, prod, mask, start, dst_start, span, unroll=2):
    def load(ref, p, t):
        return ref[p, pl.ds(start + t, 8, stride=span), :]

    def line(j, p, t):
        return prod[j, p, pl.ds(start + t, 8, stride=span), :]

    def density(t, k):
        return -0.25 * THERMAL * load(src, k, t) + 0.25 * HALINE * load(src, K + k, t)

    def pressures(t):
        out = [density(t, 0)]
        for k in range(1, K):
            out.append(out[-1] + density(t, k))
        return out

    def fluxes(t):
        out = [None] * STATE
        for k in range(K):
            speed = None
            for f in (3, 0, 1, 2):
                p = f * K + k
                a = load(src, p, t) + load(src, p, t + 1)
                value = 7.0 * a - (load(src, p, t - 1) + load(src, p, t + 2))
                if f == 3:
                    speed = a
                out[p] = speed * value
        return out

    def row(t, carry):
        below_flux, p_prev, p_here = carry
        wet = coef(STATE + K, t) * mask
        wet24 = wet * (1.0 / 24.0)
        wet_cor = wet * cor[pl.ds(start + t, 8, stride=span), :]
        p_next = pressures(t + 1)
        above = fluxes(t)
        grad_lon = None
        for k in range(K):
            wet_mix = wet * coef(STATE + k, t)
            drop = -0.25 * THERMAL * line(3, k, t) + 0.25 * HALINE * line(3, K + k, t)
            grad_lon = drop if k == 0 else grad_lon + drop
            u = load(src, 2 * K + k, t)
            mean = 3.0 * u + 0.5 * line(2, 2 * K + k, t)
            half = 0.5 * line(3, 2 * K + k, t)
            east_speed, west_speed = mean + half, mean - half
            for f in range(4):
                p = f * K + k
                q = load(src, p, t)
                adv = (east_speed * line(0, p, t) - west_speed * line(1, p, t)) + (above[p] - below_flux[p])
                lap = line(2, p, t) + (load(src, p, t + 1) + load(src, p, t - 1))
                if f < 2:
                    if 0 < k < K - 1:
                        lap = lap + (0.5 * (load(src, p - 1, t) + load(src, p + 1, t)) - q)
                    elif k == 0:
                        lap = lap + 0.5 * (load(src, p + 1, t) - q)
                    else:
                        lap = lap + 0.5 * (load(src, p - 1, t) - q)
                new = q + (wet_mix * lap - wet24 * adv)
                if f == 2:
                    new = new + (wet_cor * load(src, p + K, t) - wet * grad_lon)
                if f == 3:
                    new = new - (wet_cor * load(src, p - K, t) + wet * (p_next[k] - p_prev[k]))
                dst[p, pl.ds(dst_start + t, 8, stride=span), :] = new
        return above, p_here, p_next

    init = (fluxes(-1), pressures(-1), pressures(0))
    lax.fori_loop(0, span, row, init, unroll=unroll)


def window(tile, cor, seams, weights, prod, even, odd, out):
    span_rows = tile.shape[1] - 2 * PAD
    lane = lax.broadcasted_iota(jnp.int32, (8, LANES), 1)
    room = jnp.full((8, LANES), LANES, jnp.int32)
    for seam in seams:
        after = lax.rem(lane - seam + LANES, LANES)
        room = jnp.minimum(room, jnp.minimum(after, LANES - 1 - after))
    src = tile
    for s in range(STEPS):
        span = SPANS[s]
        need = span_rows - 4 * (s + 1)
        spare = (8 * span - need) // 2
        start = PAD + 2 * (s + 1) - spare
        dst = out if s == STEPS - 1 else (even if s % 2 == 0 else odd)
        dst_start = PAD - spare if s == STEPS - 1 else start
        first = start // 16 * 16
        count = -(-(start + 8 * span) // 16) * 16 - first
        products(src, weights, prod, first, count)

        def coef(p, t, start=start, span=span):
            return tile[p, pl.ds(start + t, 8, stride=span), :]

        mask = jnp.where(room >= 2 * (s + 1), 1.0, 0.0)
        substep(src, dst, coef, cor, prod, mask, start, dst_start, span)
        src = dst


def interior_kernel(tiles, cor, out, even, odd, weights, prod):
    weights[...] = line_weights()

    @pl.loop(0, 2)
    def _(i):
        window(tiles.at[i], cor, (96 * i,), weights, prod, even, odd, out.at[i])


def interior(tiles, cor):
    rows = tiles.shape[2]
    block = rows - 2 * PAD - 2 * HALO
    vmem = pl.BlockSpec(memory_space=pltpu.VMEM)
    cells = 2 * STATE * rows * LANES
    return pl.pallas_call(
        interior_kernel,
        in_specs=[pl.BlockSpec((2,) + tiles.shape[1:], lambda g: (0, 0, 0, 0)), pl.BlockSpec(cor.shape, lambda g: (0, 0))],
        out_specs=pl.BlockSpec((2, STATE, block + 2 * PAD, LANES), lambda g: (0, 0, 0, 0)),
        grid=(1,),
        out_shape=jax.ShapeDtypeStruct((2, STATE, block + 2 * PAD, LANES), jnp.float32),
        scratch_shapes=[
            pltpu.VMEM((STATE, rows, LANES), jnp.float32),
            pltpu.VMEM((STATE, rows, LANES), jnp.float32),
            pltpu.VMEM((2 * LANES, 4 * LANES), jnp.bfloat16),
            pltpu.VMEM((4, STATE, rows, LANES), jnp.float32),
        ],
        compiler_params=params(),
        cost_estimate=pl.CostEstimate(flops=STEPS * 30 * cells, transcendentals=0, bytes_accessed=8 * cells),
        name="interior",
    )(tiles, cor)


def edge_kernel(tiles, cor, got_low, got_high, inner, out, tile, even, odd, edge, weights, prod):
    span = got_low.shape[1]
    block = out.shape[1]
    weights[...] = line_weights()

    @pl.loop(0, span // 8)
    def _(g):
        r = pl.multiple_of(g * 8, 8)
        lane = lax.broadcasted_iota(jnp.int32, (8, LANES), 1)
        for p in range(PLANES):
            left = shifted(got_low[p // 8, pl.ds(r, 8)], 16 - 16 * (p % 8))
            right = shifted(got_high[p // 8, pl.ds(r, 8)], -16 * (p % 8))
            mid = tiles[0, p, pl.ds(PAD + r, 8)]
            tile[p, pl.ds(PAD + r, 8)] = jnp.where(lane < 16, right, jnp.where(lane < 32, left, mid))

    window(tile, cor, (16, 64), weights, prod, even, odd, edge)

    @pl.loop(0, block // 8)
    def _(g):
        r = pl.multiple_of(g * 8, 8)
        lane = lax.broadcasted_iota(jnp.int32, (8, LANES), 1)
        for p in range(STATE):
            here = pl.ds(PAD + r, 8)
            e = edge[p, here]
            lo = inner[0, p, here]
            hi = inner[1, p, here]
            out[p, pl.ds(r, 8), :LANES] = jnp.where(lane < 16, shifted(e, -32), jnp.where(lane < 112, lo, hi))
            out[p, pl.ds(r, 8), LANES:] = jnp.where(lane < 80, hi, e)


def edges(tiles, cor, got_low, got_high, inner, cols):
    rows = tiles.shape[2]
    block = rows - 2 * PAD - 2 * HALO
    whole = lambda a: pl.BlockSpec(a.shape, functools.partial(lambda n, g: (0,) * n, len(a.shape)))
    f32 = jnp.float32
    shape = jax.ShapeDtypeStruct((STATE, block, cols), f32)
    return pl.pallas_call(
        edge_kernel,
        grid=(1,),
        in_specs=[pl.BlockSpec((1,) + tiles.shape[1:], lambda g: (2, 0, 0, 0)), whole(cor), whole(got_low), whole(got_high), whole(inner)],
        out_specs=whole(shape),
        out_shape=shape,
        scratch_shapes=[
            pltpu.VMEM((PLANES, rows, LANES), f32),
            pltpu.VMEM((STATE, rows, LANES), f32),
            pltpu.VMEM((STATE, rows, LANES), f32),
            pltpu.VMEM((STATE, block + 2 * PAD, LANES), f32),
            pltpu.VMEM((2 * LANES, 4 * LANES), jnp.bfloat16),
            pltpu.VMEM((4, STATE, rows, LANES), f32),
        ],
        compiler_params=params(),
        name="edges",
    )(tiles, cor, got_low, got_high, inner)


def body(ocean_state, mixing, land_sea):
    block, cols = land_sea.shape
    n_lon, n_lat = lax.axis_size("lon"), lax.axis_size("lat")
    axes = ("lon", "lat")

    def at(i, l):
        return (i % n_lon) * n_lat + l

    pairs_b = [(at(i, l), at(i, l ^ 1)) for i in range(n_lon) for l in range(n_lat)]
    pairs_a = []
    for i in range(n_lon):
        for l in range(1, n_lat - 1, 2):
            pairs_a += [(at(i, l), at(i, l + 1)), (at(i, l + 1), at(i, l))]
        pairs_a.append((at(i, n_lat - 1), at(n_lon - 1 - i, n_lat - 1)))
    east = [(i, (i + 1) % n_lon) for i in range(n_lon)]
    west = [((i + 1) % n_lon, i) for i in range(n_lon)]

    x = ocean_state.reshape(STATE, block, cols)
    to_a, to_b = pack_rows(x, mixing, land_sea)
    ra = lax.ppermute(to_a, axes, pairs_a)
    rb = lax.ppermute(to_b, axes, pairs_b)
    tiles, send_low, send_high, cor = extend(x, mixing, land_sea, ra, rb)
    got_low = lax.ppermute(send_high, "lon", east)
    got_high = lax.ppermute(send_low, "lon", west)
    inner = interior(tiles, cor)
    out = edges(tiles, cor, got_low, got_high, inner, cols)
    return out.reshape(ocean_state.shape)


def solution(mesh):
    in_specs = (P(None, None, "lat", "lon"), P(None, "lat", "lon"), P("lat", "lon"))
    out_specs = P(None, None, "lat", "lon")
    return jax.shard_map(body, mesh=mesh, in_specs=in_specs, out_specs=out_specs, check_vma=False)
```

```python
import functools
import jax
import jax.numpy as jnp
from jax import lax
from jax.experimental import pallas as pl
from jax.experimental.pallas import tpu as pltpu
from jax.sharding import PartitionSpec as P

STEPS = 8
K = 3
HALO = 2 * STEPS
LANES = 128
PAD = 8

THERMAL = 0.2
HALINE = 0.15
GRAVITY = 0.5
TIMESTEP = 0.1

STATE = 4 * K
PLANES = STATE + K + 1
VMEM_LIMIT = 24 * 1024 * 1024
SPANS = (21, 19, 19, 19, 19, 17, 17, 17)


def params():
    return pltpu.CompilerParams(vmem_limit_bytes=VMEM_LIMIT)


def shifted(x, by):
    return pltpu.roll(x, by % LANES, 1)


def pack_rows_kernel(x, m, w, to_a, to_b, wet, sems):
    even = lax.rem(lax.axis_index("lat"), 2) == 0
    last = x.shape[1] - HALO
    starts = (jnp.where(even, 0, last), jnp.where(even, last, 0))
    copies = []
    for i, dest in enumerate((to_a, to_b)):
        rows = pl.ds(pl.multiple_of(starts[i], HALO), HALO)
        copies.append(pltpu.make_async_copy(x.at[:, rows, :], dest.at[pl.ds(0, STATE)], sems.at[3 * i]))
        copies.append(pltpu.make_async_copy(m.at[:, rows, :], dest.at[pl.ds(STATE, K)], sems.at[3 * i + 1]))
        copies.append(pltpu.make_async_copy(w.at[rows, :], wet.at[i], sems.at[3 * i + 2]))
    for copy in copies:
        copy.start()
    for copy in copies:
        copy.wait()
    for i, dest in enumerate((to_a, to_b)):
        dest[STATE + K] = TIMESTEP * wet[i].astype(jnp.float32)


def pack_rows(x, mixing, land):
    cols = land.shape[1]
    slab = jax.ShapeDtypeStruct((PLANES, HALO, cols), jnp.float32)
    return pl.pallas_call(
        pack_rows_kernel,
        in_specs=[pl.BlockSpec(memory_space=pltpu.HBM)] * 3,
        out_specs=[pl.BlockSpec(memory_space=pltpu.VMEM)] * 2,
        out_shape=[slab, slab],
        scratch_shapes=[pltpu.VMEM((2, HALO, cols), jnp.int32), pltpu.SemaphoreType.DMA((6,))],
        compiler_params=params(),
        name="pack_rows",
    )(x, mixing, land)


def fold(slab):
    planes, rows, cols = slab.shape
    flat = slab.reshape(planes * rows, cols)
    n = planes * rows
    i = lax.broadcasted_iota(jnp.int32, (n, n), 0)
    j = lax.broadcasted_iota(jnp.int32, (n, n), 1)
    plane = i // rows
    sign = jnp.where(jnp.logical_and(plane >= 2 * K, plane < STATE), -1.0, 1.0)
    left = jnp.where(j == plane * rows + (rows - 1 - (i - plane * rows)), sign, 0.0).astype(jnp.float32)
    a = lax.broadcasted_iota(jnp.int32, (cols, cols), 0)
    b = lax.broadcasted_iota(jnp.int32, (cols, cols), 1)
    right = jnp.where(a + b == cols - 1, 1.0, 0.0).astype(jnp.float32)
    dot = functools.partial(jnp.dot, precision=lax.Precision.HIGHEST, preferred_element_type=jnp.float32)
    return dot(dot(left, flat), right).reshape(slab.shape)


def place(at, source, tiles, send_low, send_high):
    lane = lax.broadcasted_iota(jnp.int32, (8, LANES), 1)
    for group in range(PLANES // 8):
        low = jnp.zeros((8, LANES), jnp.float32)
        high = jnp.zeros((8, LANES), jnp.float32)
        for q in range(8):
            p = group * 8 + q
            lo, hi = source(p)
            here = pl.ds(PAD + at, 8)
            tiles[0][p, here] = lo
            tiles[1][p, here] = jnp.where(lane < 96, hi, lo)
            tiles[2][p, here] = jnp.where(lane < 64, shifted(lo, 32), hi)
            mine = jnp.logical_and(lane >= 16 * q, lane < 16 * q + 16)
            low = jnp.where(mine, shifted(lo, 16 * q), low)
            high = jnp.where(mine, shifted(hi, 16 * q - 112), high)
        send_low[group, pl.ds(at, 8)] = low
        send_high[group, pl.ds(at, 8)] = high


def extend_kernel(x_all, m_all, w_all, tile0, tile1, tile2, send_low, send_high, cor, x, m, w, sems):
    pairs = ((x_all, x), (m_all, m), (w_all, w))
    copies = [pltpu.make_async_copy(a, b, sems.at[i]) for i, (a, b) in enumerate(pairs)]
    for copy in copies:
        copy.start()
    lat = lax.axis_index("lat")
    block = x.shape[1]
    total = block * lax.axis_size("lat")
    row = lax.broadcasted_iota(jnp.int32, cor.shape, 0) + (lat * block - HALO - PAD)
    cor[...] = jnp.sin(jnp.pi * (row.astype(jnp.float32) + 0.5) / total - jnp.pi / 2)
    for copy in copies:
        copy.wait()

    @pl.loop(0, block // 8)
    def _(g):
        r = pl.multiple_of(g * 8, 8)

        def source(p):
            if p < STATE:
                return x[p, pl.ds(r, 8), :LANES], x[p, pl.ds(r, 8), LANES:]
            if p < STATE + K:
                return m[p - STATE, pl.ds(r, 8), :LANES], m[p - STATE, pl.ds(r, 8), LANES:]
            return (
                TIMESTEP * w[pl.ds(r, 8), :LANES].astype(jnp.float32),
                TIMESTEP * w[pl.ds(r, 8), LANES:].astype(jnp.float32),
            )

        place(HALO + r, source, (tile0, tile1, tile2), send_low, send_high)


def halo_rows_kernel(ra, rb, t0, t1, t2, sl, sh, tile0, tile1, tile2, send_low, send_high, folded):
    del t0, t1, t2, sl, sh
    lat = lax.axis_index("lat")
    north_at = tile0.shape[1] - 2 * PAD - HALO

    def put(at, slab):
        for r in range(0, HALO, 8):

            def source(p, r=r):
                return slab[p, pl.ds(r, 8), :LANES], slab[p, pl.ds(r, 8), LANES:]

            place(at + r, source, (tile0, tile1, tile2), send_low, send_high)

    @pl.when(lax.rem(lat, 2) == 0)
    def _():
        put(0, ra)
        put(north_at, rb)

    @pl.when(lax.rem(lat, 2) == 1)
    def _():
        put(0, rb)

        @pl.when(lat == lax.axis_size("lat") - 1)
        def _():
            folded[...] = fold(ra[...])

        @pl.when(lat != lax.axis_size("lat") - 1)
        def _():
            folded[...] = ra[...]

        put(north_at, folded)


def extend(x, mixing, land):
    block = land.shape[0]
    span = block + 2 * HALO
    f32 = jnp.float32
    vmem = pl.BlockSpec(memory_space=pltpu.VMEM)
    tile = jax.ShapeDtypeStruct((PLANES, span + 2 * PAD, LANES), f32)
    send = jax.ShapeDtypeStruct((PLANES // 8, span, LANES), f32)
    return pl.pallas_call(
        extend_kernel,
        in_specs=[pl.BlockSpec(memory_space=pltpu.HBM)] * 3,
        out_specs=[vmem] * 6,
        out_shape=[tile, tile, tile, send, send, jax.ShapeDtypeStruct((span + 2 * PAD, LANES), f32)],
        scratch_shapes=[
            pltpu.VMEM(x.shape, f32),
            pltpu.VMEM(mixing.shape, f32),
            pltpu.VMEM(land.shape, jnp.int32),
            pltpu.SemaphoreType.DMA((3,)),
        ],
        compiler_params=params(),
        name="extend",
    )(x, mixing, land)


def halo_rows(ra, rb, *parts):
    vmem = pl.BlockSpec(memory_space=pltpu.VMEM)
    return pl.pallas_call(
        halo_rows_kernel,
        in_specs=[vmem] * 7,
        out_specs=[vmem] * 5,
        out_shape=[jax.ShapeDtypeStruct(part.shape, part.dtype) for part in parts],
        input_output_aliases={i + 2: i for i in range(5)},
        scratch_shapes=[pltpu.VMEM(ra.shape, jnp.float32)],
        compiler_params=params(),
        name="halo_rows",
    )(ra, rb, *parts)


def line_weights():
    shape = (2 * LANES, LANES)
    here = lax.rem(lax.broadcasted_iota(jnp.int32, shape, 0), LANES)
    lane = lax.broadcasted_iota(jnp.int32, shape, 1)
    gap = lax.rem(here - lane + LANES, LANES)

    def stencil(terms):
        out = jnp.zeros(shape, jnp.float32)
        for offset, value in terms:
            out = jnp.where(gap == offset % LANES, value, out)
        return out

    east = stencil(((0, 7.0), (1, 7.0), (-1, -1.0), (2, -1.0)))
    west = stencil(((-1, 7.0), (0, 7.0), (-2, -1.0), (1, -1.0)))
    lap = stencil(((0, -4.0), (1, 1.0), (-1, 1.0)))
    diff = stencil(((1, 1.0), (-1, -1.0)))
    return jnp.concatenate([east, west, lap, diff], axis=1).astype(jnp.bfloat16)


def products(src, weights, prod, first, count):
    for f in range(4):
        planes = pl.ds(f * K, K)
        rows = pl.ds(first, count)
        q = src[planes, rows, :].reshape(K * count, LANES)
        high = q.astype(jnp.bfloat16)
        low = (q - high.astype(jnp.float32)).astype(jnp.bfloat16)
        both = jnp.concatenate([high, low], axis=1)
        got = jnp.dot(both, weights[...], preferred_element_type=jnp.float32)
        for j in range(4 if f < 3 else 3):
            prod[j, planes, rows, :] = got[:, j * LANES : (j + 1) * LANES].reshape(K, count, LANES)


def substep(src, dst, coef, cor, prod, mask, start, dst_start, span, unroll=2):
    def load(ref, p, t):
        return ref[p, pl.ds(start + t, 8, stride=span), :]

    def line(j, p, t):
        return prod[j, p, pl.ds(start + t, 8, stride=span), :]

    def density(t, k):
        return -0.25 * THERMAL * load(src, k, t) + 0.25 * HALINE * load(src, K + k, t)

    def pressures(t):
        out = [density(t, 0)]
        for k in range(1, K):
            out.append(out[-1] + density(t, k))
        return out

    def fluxes(t):
        out = [None] * STATE
        for k in range(K):
            speed = None
            for f in (3, 0, 1, 2):
                p = f * K + k
                a = load(src, p, t) + load(src, p, t + 1)
                value = 7.0 * a - (load(src, p, t - 1) + load(src, p, t + 2))
                if f == 3:
                    speed = a
                out[p] = speed * value
        return out

    def row(t, carry):
        below_flux, p_prev, p_here = carry
        wet = coef(STATE + K, t) * mask
        wet24 = wet * (1.0 / 24.0)
        wet_cor = wet * cor[pl.ds(start + t, 8, stride=span), :]
        p_next = pressures(t + 1)
        above = fluxes(t)
        grad_lon = None
        for k in range(K):
            wet_mix = wet * coef(STATE + k, t)
            drop = -0.25 * THERMAL * line(3, k, t) + 0.25 * HALINE * line(3, K + k, t)
            grad_lon = drop if k == 0 else grad_lon + drop
            u = load(src, 2 * K + k, t)
            mean = 3.0 * u + 0.5 * line(2, 2 * K + k, t)
            half = 0.5 * line(3, 2 * K + k, t)
            east_speed, west_speed = mean + half, mean - half
            for f in range(4):
                p = f * K + k
                q = load(src, p, t)
                adv = (east_speed * line(0, p, t) - west_speed * line(1, p, t)) + (above[p] - below_flux[p])
                lap = line(2, p, t) + (load(src, p, t + 1) + load(src, p, t - 1))
                if f < 2:
                    if 0 < k < K - 1:
                        lap = lap + (0.5 * (load(src, p - 1, t) + load(src, p + 1, t)) - q)
                    elif k == 0:
                        lap = lap + 0.5 * (load(src, p + 1, t) - q)
                    else:
                        lap = lap + 0.5 * (load(src, p - 1, t) - q)
                new = q + (wet_mix * lap - wet24 * adv)
                if f == 2:
                    new = new + (wet_cor * load(src, p + K, t) - wet * grad_lon)
                if f == 3:
                    new = new - (wet_cor * load(src, p - K, t) + wet * (p_next[k] - p_prev[k]))
                dst[p, pl.ds(dst_start + t, 8, stride=span), :] = new
        return above, p_here, p_next

    init = (fluxes(-1), pressures(-1), pressures(0))
    lax.fori_loop(0, span, row, init, unroll=unroll)


def window(tile, cor, seams, weights, prod, even, odd, out):
    span_rows = tile.shape[1] - 2 * PAD
    lane = lax.broadcasted_iota(jnp.int32, (8, LANES), 1)
    room = jnp.full((8, LANES), LANES, jnp.int32)
    for seam in seams:
        after = lax.rem(lane - seam + LANES, LANES)
        room = jnp.minimum(room, jnp.minimum(after, LANES - 1 - after))
    src = tile
    for s in range(STEPS):
        span = SPANS[s]
        need = span_rows - 4 * (s + 1)
        spare = (8 * span - need) // 2
        start = PAD + 2 * (s + 1) - spare
        dst = out if s == STEPS - 1 else (even if s % 2 == 0 else odd)
        dst_start = PAD - spare if s == STEPS - 1 else start
        first = start // 16 * 16
        count = -(-(start + 8 * span) // 16) * 16 - first
        products(src, weights, prod, first, count)

        def coef(p, t, start=start, span=span):
            return tile[p, pl.ds(start + t, 8, stride=span), :]

        mask = jnp.where(room >= 2 * (s + 1), 1.0, 0.0)
        substep(src, dst, coef, cor, prod, mask, start, dst_start, span)
        src = dst


def interior_kernel(seam, tile, cor, out, even, odd, weights, prod):
    weights[...] = line_weights()
    window(tile, cor, (seam,), weights, prod, even, odd, out)


def interior(tile, cor, seam):
    rows = tile.shape[1]
    block = rows - 2 * PAD - 2 * HALO
    vmem = pl.BlockSpec(memory_space=pltpu.VMEM)
    f32 = jnp.float32
    return pl.pallas_call(
        functools.partial(interior_kernel, seam),
        in_specs=[vmem, vmem],
        out_specs=vmem,
        out_shape=jax.ShapeDtypeStruct((STATE, block + 2 * PAD, LANES), f32),
        scratch_shapes=[
            pltpu.VMEM((STATE, rows, LANES), f32),
            pltpu.VMEM((STATE, rows, LANES), f32),
            pltpu.VMEM((2 * LANES, 4 * LANES), jnp.bfloat16),
            pltpu.VMEM((4, STATE, rows, LANES), f32),
        ],
        compiler_params=params(),
        name="interior",
    )(tile, cor)


def edge_kernel(start, cor, got_low, got_high, inner0, inner1, out, tile, even, odd, edge, weights, prod):
    span = got_low.shape[1]
    block = out.shape[1]
    weights[...] = line_weights()

    @pl.loop(0, span // 8)
    def _(g):
        r = pl.multiple_of(g * 8, 8)
        lane = lax.broadcasted_iota(jnp.int32, (8, LANES), 1)
        for p in range(PLANES):
            left = shifted(got_low[p // 8, pl.ds(r, 8)], 16 - 16 * (p % 8))
            right = shifted(got_high[p // 8, pl.ds(r, 8)], -16 * (p % 8))
            mid = start[p, pl.ds(PAD + r, 8)]
            tile[p, pl.ds(PAD + r, 8)] = jnp.where(lane < 16, right, jnp.where(lane < 32, left, mid))

    window(tile, cor, (16, 64), weights, prod, even, odd, edge)

    @pl.loop(0, block // 8)
    def _(g):
        r = pl.multiple_of(g * 8, 8)
        lane = lax.broadcasted_iota(jnp.int32, (8, LANES), 1)
        for p in range(STATE):
            here = pl.ds(PAD + r, 8)
            e = edge[p, here]
            lo = inner0[p, here]
            hi = inner1[p, here]
            out[p, pl.ds(r, 8), :LANES] = jnp.where(lane < 16, shifted(e, -32), jnp.where(lane < 112, lo, hi))
            out[p, pl.ds(r, 8), LANES:] = jnp.where(lane < 80, hi, e)


def edges(start, cor, got_low, got_high, inner0, inner1):
    rows = start.shape[1]
    block = rows - 2 * PAD - 2 * HALO
    f32 = jnp.float32
    vmem = pl.BlockSpec(memory_space=pltpu.VMEM)
    return pl.pallas_call(
        edge_kernel,
        in_specs=[vmem] * 6,
        out_specs=vmem,
        out_shape=jax.ShapeDtypeStruct((STATE, block, 2 * LANES), f32),
        scratch_shapes=[
            pltpu.VMEM((PLANES, rows, LANES), f32),
            pltpu.VMEM((STATE, rows, LANES), f32),
            pltpu.VMEM((STATE, rows, LANES), f32),
            pltpu.VMEM((STATE, block + 2 * PAD, LANES), f32),
            pltpu.VMEM((2 * LANES, 4 * LANES), jnp.bfloat16),
            pltpu.VMEM((4, STATE, rows, LANES), f32),
        ],
        compiler_params=params(),
        name="edges",
    )(start, cor, got_low, got_high, inner0, inner1)


def body(ocean_state, mixing, land_sea):
    block, cols = land_sea.shape
    n_lon, n_lat = lax.axis_size("lon"), lax.axis_size("lat")
    axes = ("lon", "lat")

    def at(i, l):
        return (i % n_lon) * n_lat + l

    pairs_b = [(at(i, l), at(i, l ^ 1)) for i in range(n_lon) for l in range(n_lat)]
    pairs_a = []
    for i in range(n_lon):
        for l in range(1, n_lat - 1, 2):
            pairs_a += [(at(i, l), at(i, l + 1)), (at(i, l + 1), at(i, l))]
        pairs_a.append((at(i, n_lat - 1), at(n_lon - 1 - i, n_lat - 1)))
    east = [(i, (i + 1) % n_lon) for i in range(n_lon)]
    west = [((i + 1) % n_lon, i) for i in range(n_lon)]

    x = ocean_state.reshape(STATE, block, cols)
    to_a, to_b = pack_rows(x, mixing, land_sea)
    ra = lax.ppermute(to_a, axes, pairs_a)
    rb = lax.ppermute(to_b, axes, pairs_b)
    *parts, cor = extend(x, mixing, land_sea)
    tile0, tile1, tile2, send_low, send_high = halo_rows(ra, rb, *parts)
    inner0 = interior(tile0, cor, 0)
    send_low, send_high, inner0 = lax.optimization_barrier((send_low, send_high, inner0))
    got_low = lax.ppermute(send_high, "lon", east)
    got_high = lax.ppermute(send_low, "lon", west)
    inner1 = interior(tile1, cor, 96)
    out = edges(tile2, cor, got_low, got_high, inner0, inner1)
    return out.reshape(ocean_state.shape)


def solution(mesh):
    in_specs = (P(None, None, "lat", "lon"), P(None, "lat", "lon"), P("lat", "lon"))
    out_specs = P(None, None, "lat", "lon")
    return jax.shard_map(body, mesh=mesh, in_specs=in_specs, out_specs=out_specs, check_vma=False)
```

```python
import functools
import jax
import jax.numpy as jnp
from jax import lax
from jax.experimental import pallas as pl
from jax.experimental.pallas import tpu as pltpu
from jax.sharding import PartitionSpec as P

STEPS = 8
K = 3
HALO = 2 * STEPS
LANES = 128
PAD = 8

THERMAL = 0.2
HALINE = 0.15
GRAVITY = 0.5
TIMESTEP = 0.1

STATE = 4 * K
PLANES = STATE + K + 1
VMEM_LIMIT = 24 * 1024 * 1024
SPANS = (21, 19, 19, 19, 19, 17, 17, 17)


def params():
    return pltpu.CompilerParams(vmem_limit_bytes=VMEM_LIMIT)


def shifted(x, by):
    return pltpu.roll(x, by % LANES, 1)


def pack_rows_kernel(x, m, w, to_a, to_b, wet, sems):
    even = lax.rem(lax.axis_index("lat"), 2) == 0
    last = x.shape[1] - HALO
    starts = (jnp.where(even, 0, last), jnp.where(even, last, 0))
    copies = []
    for i, dest in enumerate((to_a, to_b)):
        rows = pl.ds(pl.multiple_of(starts[i], HALO), HALO)
        copies.append(pltpu.make_async_copy(x.at[:, rows, :], dest.at[pl.ds(0, STATE)], sems.at[3 * i]))
        copies.append(pltpu.make_async_copy(m.at[:, rows, :], dest.at[pl.ds(STATE, K)], sems.at[3 * i + 1]))
        copies.append(pltpu.make_async_copy(w.at[rows, :], wet.at[i], sems.at[3 * i + 2]))
    for copy in copies:
        copy.start()
    for copy in copies:
        copy.wait()
    for i, dest in enumerate((to_a, to_b)):
        dest[STATE + K] = TIMESTEP * wet[i].astype(jnp.float32)


def pack_rows(x, mixing, land):
    cols = land.shape[1]
    slab = jax.ShapeDtypeStruct((PLANES, HALO, cols), jnp.float32)
    return pl.pallas_call(
        pack_rows_kernel,
        in_specs=[pl.BlockSpec(memory_space=pltpu.HBM)] * 3,
        out_specs=[pl.BlockSpec(memory_space=pltpu.VMEM)] * 2,
        out_shape=[slab, slab],
        scratch_shapes=[pltpu.VMEM((2, HALO, cols), jnp.int32), pltpu.SemaphoreType.DMA((6,))],
        compiler_params=params(),
        name="pack_rows",
    )(x, mixing, land)


def fold(slab):
    planes, rows, cols = slab.shape
    flat = slab.reshape(planes * rows, cols)
    n = planes * rows
    i = lax.broadcasted_iota(jnp.int32, (n, n), 0)
    j = lax.broadcasted_iota(jnp.int32, (n, n), 1)
    plane = i // rows
    sign = jnp.where(jnp.logical_and(plane >= 2 * K, plane < STATE), -1.0, 1.0)
    left = jnp.where(j == plane * rows + (rows - 1 - (i - plane * rows)), sign, 0.0).astype(jnp.float32)
    a = lax.broadcasted_iota(jnp.int32, (cols, cols), 0)
    b = lax.broadcasted_iota(jnp.int32, (cols, cols), 1)
    right = jnp.where(a + b == cols - 1, 1.0, 0.0).astype(jnp.float32)
    dot = functools.partial(jnp.dot, precision=lax.Precision.HIGHEST, preferred_element_type=jnp.float32)
    return dot(dot(left, flat), right).reshape(slab.shape)


def place(at, source, tiles, send_low, send_high):
    lane = lax.broadcasted_iota(jnp.int32, (8, LANES), 1)
    for group in range(PLANES // 8):
        low = jnp.zeros((8, LANES), jnp.float32)
        high = jnp.zeros((8, LANES), jnp.float32)
        for q in range(8):
            p = group * 8 + q
            lo, hi = source(p)
            here = pl.ds(PAD + at, 8)
            tiles[0][p, here] = lo
            tiles[1][p, here] = jnp.where(lane < 96, hi, lo)
            tiles[2][p, here] = jnp.where(lane < 64, shifted(lo, 32), hi)
            slot = 16 * ((q + 1) % 8)
            low = jnp.where(jnp.logical_and(lane >= 16 * q, lane < 16 * q + 16), shifted(lo, 16 * q), low)
            high = jnp.where(jnp.logical_and(lane >= slot, lane < slot + 16), shifted(hi, slot - 112), high)
        send_low[group, pl.ds(at, 8)] = low
        send_high[group, pl.ds(at, 8)] = high


def extend_kernel(x_all, m_all, w_all, tile0, tile1, tile2, send_low, send_high, cor, weights, x, m, w, sems):
    pairs = ((x_all, x), (m_all, m), (w_all, w))
    copies = [pltpu.make_async_copy(a, b, sems.at[i]) for i, (a, b) in enumerate(pairs)]
    for copy in copies:
        copy.start()
    weights[...] = line_weights()
    lat = lax.axis_index("lat")
    block = x.shape[1]
    total = block * lax.axis_size("lat")
    row = lax.broadcasted_iota(jnp.int32, cor.shape, 0) + (lat * block - HALO - PAD)
    cor[...] = jnp.sin(jnp.pi * (row.astype(jnp.float32) + 0.5) / total - jnp.pi / 2)
    for copy in copies:
        copy.wait()

    @pl.loop(0, block // 8)
    def _(g):
        r = pl.multiple_of(g * 8, 8)

        def source(p):
            if p < STATE:
                return x[p, pl.ds(r, 8), :LANES], x[p, pl.ds(r, 8), LANES:]
            if p < STATE + K:
                return m[p - STATE, pl.ds(r, 8), :LANES], m[p - STATE, pl.ds(r, 8), LANES:]
            return (
                TIMESTEP * w[pl.ds(r, 8), :LANES].astype(jnp.float32),
                TIMESTEP * w[pl.ds(r, 8), LANES:].astype(jnp.float32),
            )

        place(HALO + r, source, (tile0, tile1, tile2), send_low, send_high)


def halo_rows_kernel(ra, rb, t0, t1, t2, sl, sh, tile0, tile1, tile2, send_low, send_high, folded):
    del t0, t1, t2, sl, sh
    lat = lax.axis_index("lat")
    north_at = tile0.shape[1] - 2 * PAD - HALO

    def put(at, slab):
        for r in range(0, HALO, 8):

            def source(p, r=r):
                return slab[p, pl.ds(r, 8), :LANES], slab[p, pl.ds(r, 8), LANES:]

            place(at + r, source, (tile0, tile1, tile2), send_low, send_high)

    @pl.when(lax.rem(lat, 2) == 0)
    def _():
        put(0, ra)
        put(north_at, rb)

    @pl.when(lax.rem(lat, 2) == 1)
    def _():
        put(0, rb)

        @pl.when(lat == lax.axis_size("lat") - 1)
        def _():
            folded[...] = fold(ra[...])

        @pl.when(lat != lax.axis_size("lat") - 1)
        def _():
            folded[...] = ra[...]

        put(north_at, folded)


def extend(x, mixing, land):
    block = land.shape[0]
    span = block + 2 * HALO
    f32 = jnp.float32
    vmem = pl.BlockSpec(memory_space=pltpu.VMEM)
    tile = jax.ShapeDtypeStruct((PLANES, span + 2 * PAD, LANES), f32)
    send = jax.ShapeDtypeStruct((PLANES // 8, span, LANES), f32)
    return pl.pallas_call(
        extend_kernel,
        in_specs=[pl.BlockSpec(memory_space=pltpu.HBM)] * 3,
        out_specs=[vmem] * 7,
        out_shape=[
            tile,
            tile,
            tile,
            send,
            send,
            jax.ShapeDtypeStruct((span + 2 * PAD, LANES), f32),
            jax.ShapeDtypeStruct((2 * LANES, 4 * LANES), jnp.bfloat16),
        ],
        scratch_shapes=[
            pltpu.VMEM(x.shape, f32),
            pltpu.VMEM(mixing.shape, f32),
            pltpu.VMEM(land.shape, jnp.int32),
            pltpu.SemaphoreType.DMA((3,)),
        ],
        compiler_params=params(),
        name="extend",
    )(x, mixing, land)


def halo_rows(ra, rb, *parts):
    vmem = pl.BlockSpec(memory_space=pltpu.VMEM)
    return pl.pallas_call(
        halo_rows_kernel,
        in_specs=[vmem] * 7,
        out_specs=[vmem] * 5,
        out_shape=[jax.ShapeDtypeStruct(part.shape, part.dtype) for part in parts],
        input_output_aliases={i + 2: i for i in range(5)},
        scratch_shapes=[pltpu.VMEM(ra.shape, jnp.float32)],
        compiler_params=params(),
        name="halo_rows",
    )(ra, rb, *parts)


def line_weights():
    shape = (2 * LANES, LANES)
    here = lax.rem(lax.broadcasted_iota(jnp.int32, shape, 0), LANES)
    lane = lax.broadcasted_iota(jnp.int32, shape, 1)
    gap = lax.rem(here - lane + LANES, LANES)

    def stencil(terms):
        out = jnp.zeros(shape, jnp.float32)
        for offset, value in terms:
            out = jnp.where(gap == offset % LANES, value, out)
        return out

    east = stencil(((0, 7.0), (1, 7.0), (-1, -1.0), (2, -1.0)))
    west = stencil(((-1, 7.0), (0, 7.0), (-2, -1.0), (1, -1.0)))
    lap = stencil(((0, -4.0), (1, 1.0), (-1, 1.0)))
    diff = stencil(((1, 1.0), (-1, -1.0)))
    return jnp.concatenate([east, west, lap, diff], axis=1).astype(jnp.bfloat16)


def products(src, weights, prod, first, count):
    for f in range(4):
        planes = pl.ds(f * K, K)
        rows = pl.ds(first, count)
        q = src[planes, rows, :].reshape(K * count, LANES)
        high = q.astype(jnp.bfloat16)
        low = (q - high.astype(jnp.float32)).astype(jnp.bfloat16)
        both = jnp.concatenate([high, low], axis=1)
        got = jnp.dot(both, weights[...], preferred_element_type=jnp.float32)
        for j in range(4 if f < 3 else 3):
            prod[j, planes, rows, :] = got[:, j * LANES : (j + 1) * LANES].reshape(K, count, LANES)


def substep(src, dst, coef, cor, prod, mask, start, dst_start, span, unroll=2):
    def load(ref, p, t):
        return ref[p, pl.ds(start + t, 8, stride=span), :]

    def line(j, p, t):
        return prod[j, p, pl.ds(start + t, 8, stride=span), :]

    def density(t, k):
        return -0.25 * THERMAL * load(src, k, t) + 0.25 * HALINE * load(src, K + k, t)

    def pressures(t):
        out = [density(t, 0)]
        for k in range(1, K):
            out.append(out[-1] + density(t, k))
        return out

    def fluxes(t):
        out = [None] * STATE
        for k in range(K):
            speed = None
            for f in (3, 0, 1, 2):
                p = f * K + k
                a = load(src, p, t) + load(src, p, t + 1)
                value = 7.0 * a - (load(src, p, t - 1) + load(src, p, t + 2))
                if f == 3:
                    speed = a
                out[p] = speed * value
        return out

    def row(t, carry):
        below_flux, p_prev, p_here = carry
        wet = coef(STATE + K, t) * mask
        wet24 = wet * (1.0 / 24.0)
        wet_cor = wet * cor[pl.ds(start + t, 8, stride=span), :]
        p_next = pressures(t + 1)
        above = fluxes(t)
        grad_lon = None
        for k in range(K):
            wet_mix = wet * coef(STATE + k, t)
            drop = -0.25 * THERMAL * line(3, k, t) + 0.25 * HALINE * line(3, K + k, t)
            grad_lon = drop if k == 0 else grad_lon + drop
            u = load(src, 2 * K + k, t)
            mean = 3.0 * u + 0.5 * line(2, 2 * K + k, t)
            half = 0.5 * line(3, 2 * K + k, t)
            east_speed, west_speed = mean + half, mean - half
            for f in range(4):
                p = f * K + k
                q = load(src, p, t)
                adv = (east_speed * line(0, p, t) - west_speed * line(1, p, t)) + (above[p] - below_flux[p])
                lap = line(2, p, t) + (load(src, p, t + 1) + load(src, p, t - 1))
                if f < 2:
                    if 0 < k < K - 1:
                        lap = lap + (0.5 * (load(src, p - 1, t) + load(src, p + 1, t)) - q)
                    elif k == 0:
                        lap = lap + 0.5 * (load(src, p + 1, t) - q)
                    else:
                        lap = lap + 0.5 * (load(src, p - 1, t) - q)
                new = q + (wet_mix * lap - wet24 * adv)
                if f == 2:
                    new = new + (wet_cor * load(src, p + K, t) - wet * grad_lon)
                if f == 3:
                    new = new - (wet_cor * load(src, p - K, t) + wet * (p_next[k] - p_prev[k]))
                dst[p, pl.ds(dst_start + t, 8, stride=span), :] = new
        return above, p_here, p_next

    init = (fluxes(-1), pressures(-1), pressures(0))
    lax.fori_loop(0, span, row, init, unroll=unroll)


def window(tile, cor, seams, weights, prod, even, odd, out):
    span_rows = tile.shape[1] - 2 * PAD
    lane = lax.broadcasted_iota(jnp.int32, (8, LANES), 1)
    room = jnp.full((8, LANES), LANES, jnp.int32)
    for seam in seams:
        after = lax.rem(lane - seam + LANES, LANES)
        room = jnp.minimum(room, jnp.minimum(after, LANES - 1 - after))
    src = tile
    for s in range(STEPS):
        span = SPANS[s]
        need = span_rows - 4 * (s + 1)
        spare = (8 * span - need) // 2
        start = PAD + 2 * (s + 1) - spare
        dst = out if s == STEPS - 1 else (even if s % 2 == 0 else odd)
        dst_start = PAD - spare if s == STEPS - 1 else start
        lowest = PAD + 2 * (s + 1)
        first = lowest // 8 * 8
        count = -(-(lowest + need - first) // 16) * 16
        products(src, weights, prod, first, count)

        def coef(p, t, start=start, span=span):
            return tile[p, pl.ds(start + t, 8, stride=span), :]

        mask = jnp.where(room >= 2 * (s + 1), 1.0, 0.0)
        substep(src, dst, coef, cor, prod, mask, start, dst_start, span)
        src = dst


def interior_kernel(seam, tile, cor, weights, out, even, odd, prod):
    window(tile, cor, (seam,), weights, prod, even, odd, out)


def interior(tile, cor, weights, seam):
    rows = tile.shape[1]
    block = rows - 2 * PAD - 2 * HALO
    vmem = pl.BlockSpec(memory_space=pltpu.VMEM)
    f32 = jnp.float32
    return pl.pallas_call(
        functools.partial(interior_kernel, seam),
        in_specs=[vmem] * 3,
        out_specs=vmem,
        out_shape=jax.ShapeDtypeStruct((STATE, block + 2 * PAD, LANES), f32),
        scratch_shapes=[
            pltpu.VMEM((STATE, rows, LANES), f32),
            pltpu.VMEM((STATE, rows, LANES), f32),
            pltpu.VMEM((4, STATE, rows, LANES), f32),
        ],
        compiler_params=params(),
        name="interior",
    )(tile, cor, weights)


def edge_kernel(start, cor, weights, got_low, got_high, inner0, inner1, result, tile, even, odd, edge, prod, out, sems):
    span = got_low.shape[1]
    block = result.shape[1]

    @pl.loop(0, span // 8)
    def _(g):
        r = pl.multiple_of(g * 8, 8)
        lane = lax.broadcasted_iota(jnp.int32, (8, LANES), 1)
        for p in range(PLANES):
            q = p % 8
            mine = jnp.logical_and(lane >= 16 * q, lane < 16 * q + 16)
            both = jnp.where(mine, got_high[p // 8, pl.ds(r, 8)], got_low[p // 8, pl.ds(r, 8)])
            mid = start[p, pl.ds(PAD + r, 8)]
            tile[p, pl.ds(PAD + r, 8)] = jnp.where(lane < 32, shifted(both, -16 * q), mid)

    window(tile, cor, (16, 64), weights, prod, even, odd, edge)

    copies = []
    for p in range(STATE):

        @pl.loop(0, block // 8, unroll=4)
        def _(g, p=p):
            r = pl.multiple_of(g * 8, 8)
            lane = lax.broadcasted_iota(jnp.int32, (8, LANES), 1)
            here = pl.ds(PAD + r, 8)
            e = edge[p, here]
            lo = inner0[p, here]
            hi = inner1[p, here]
            out[p, pl.ds(r, 8), :LANES] = jnp.where(lane < 16, shifted(e, -32), jnp.where(lane < 112, lo, hi))
            out[p, pl.ds(r, 8), LANES:] = jnp.where(lane < 80, hi, e)

        copies.append(pltpu.make_async_copy(out.at[p], result.at[p], sems.at[p]))
        copies[-1].start()
    for copy in copies:
        copy.wait()


def edges(start, cor, weights, got_low, got_high, inner0, inner1):
    rows = start.shape[1]
    block = rows - 2 * PAD - 2 * HALO
    f32 = jnp.float32
    vmem = pl.BlockSpec(memory_space=pltpu.VMEM)
    return pl.pallas_call(
        edge_kernel,
        in_specs=[vmem] * 7,
        out_specs=pl.BlockSpec(memory_space=pltpu.HBM),
        out_shape=jax.ShapeDtypeStruct((STATE, block, 2 * LANES), f32),
        scratch_shapes=[
            pltpu.VMEM((PLANES, rows, LANES), f32),
            pltpu.VMEM((STATE, rows, LANES), f32),
            pltpu.VMEM((STATE, rows, LANES), f32),
            pltpu.VMEM((STATE, block + 2 * PAD, LANES), f32),
            pltpu.VMEM((4, STATE, rows, LANES), f32),
            pltpu.VMEM((STATE, block, 2 * LANES), f32),
            pltpu.SemaphoreType.DMA((STATE,)),
        ],
        compiler_params=params(),
        name="edges",
    )(start, cor, weights, got_low, got_high, inner0, inner1)


def body(ocean_state, mixing, land_sea):
    block, cols = land_sea.shape
    n_lon, n_lat = lax.axis_size("lon"), lax.axis_size("lat")
    axes = ("lon", "lat")

    def at(i, l):
        return (i % n_lon) * n_lat + l

    pairs_b = [(at(i, l), at(i, l ^ 1)) for i in range(n_lon) for l in range(n_lat)]
    pairs_a = []
    for i in range(n_lon):
        for l in range(1, n_lat - 1, 2):
            pairs_a += [(at(i, l), at(i, l + 1)), (at(i, l + 1), at(i, l))]
        pairs_a.append((at(i, n_lat - 1), at(n_lon - 1 - i, n_lat - 1)))
    east = [(i, (i + 1) % n_lon) for i in range(n_lon)]
    west = [((i + 1) % n_lon, i) for i in range(n_lon)]

    x = ocean_state.reshape(STATE, block, cols)
    x, mixing, land_sea = (pltpu.with_memory_space_constraint(v, pltpu.HBM) for v in (x, mixing, land_sea))
    to_a, to_b = pack_rows(x, mixing, land_sea)
    ra = lax.ppermute(to_a, axes, pairs_a)
    rb = lax.ppermute(to_b, axes, pairs_b)
    *parts, cor, weights = extend(x, mixing, land_sea)
    tile0, tile1, tile2, send_low, send_high = halo_rows(ra, rb, *parts)
    inner0 = interior(tile0, cor, weights, 0)
    send_low, send_high, inner0 = lax.optimization_barrier((send_low, send_high, inner0))
    got_low = lax.ppermute(send_high, "lon", east)
    got_high = lax.ppermute(send_low, "lon", west)
    inner1 = interior(tile1, cor, weights, 96)
    out = edges(tile2, cor, weights, got_low, got_high, inner0, inner1)
    return out.reshape(ocean_state.shape)


def solution(mesh):
    in_specs = (P(None, None, "lat", "lon"), P(None, "lat", "lon"), P("lat", "lon"))
    out_specs = P(None, None, "lat", "lon")
    return jax.shard_map(body, mesh=mesh, in_specs=in_specs, out_specs=out_specs, check_vma=False)
```

```python
import functools
import jax
import jax.numpy as jnp
from jax import lax
from jax.experimental import pallas as pl
from jax.experimental.pallas import tpu as pltpu
from jax.sharding import PartitionSpec as P

STEPS = 8
K = 3
HALO = 2 * STEPS
LANES = 128
PAD = 8

THERMAL = 0.2
HALINE = 0.15
GRAVITY = 0.5
TIMESTEP = 0.1

STATE = 4 * K
PLANES = STATE + K + 1
VMEM_LIMIT = 24 * 1024 * 1024
SPANS = (21, 19, 19, 19, 19, 17, 17, 17)


def params():
    return pltpu.CompilerParams(vmem_limit_bytes=VMEM_LIMIT)


def shifted(x, by):
    return pltpu.roll(x, by % LANES, 1)


def pack_rows_kernel(x, m, w, to_a, to_b, wet, sems):
    even = lax.rem(lax.axis_index("lat"), 2) == 0
    last = x.shape[1] - HALO
    starts = (jnp.where(even, 0, last), jnp.where(even, last, 0))
    copies = []
    for i, dest in enumerate((to_a, to_b)):
        rows = pl.ds(pl.multiple_of(starts[i], HALO), HALO)
        copies.append(pltpu.make_async_copy(x.at[:, rows, :], dest.at[pl.ds(0, STATE)], sems.at[3 * i]))
        copies.append(pltpu.make_async_copy(m.at[:, rows, :], dest.at[pl.ds(STATE, K)], sems.at[3 * i + 1]))
        copies.append(pltpu.make_async_copy(w.at[rows, :], wet.at[i], sems.at[3 * i + 2]))
    for copy in copies:
        copy.start()
    for copy in copies:
        copy.wait()
    for i, dest in enumerate((to_a, to_b)):
        dest[STATE + K] = TIMESTEP * wet[i].astype(jnp.float32)


def pack_rows(x, mixing, land):
    cols = land.shape[1]
    slab = jax.ShapeDtypeStruct((PLANES, HALO, cols), jnp.float32)
    return pl.pallas_call(
        pack_rows_kernel,
        in_specs=[pl.BlockSpec(memory_space=pltpu.HBM)] * 3,
        out_specs=[pl.BlockSpec(memory_space=pltpu.VMEM)] * 2,
        out_shape=[slab, slab],
        scratch_shapes=[pltpu.VMEM((2, HALO, cols), jnp.int32), pltpu.SemaphoreType.DMA((6,))],
        compiler_params=params(),
        name="pack_rows",
    )(x, mixing, land)


def fold(slab):
    planes, rows, cols = slab.shape
    flat = slab.reshape(planes * rows, cols)
    n = planes * rows
    i = lax.broadcasted_iota(jnp.int32, (n, n), 0)
    j = lax.broadcasted_iota(jnp.int32, (n, n), 1)
    plane = i // rows
    sign = jnp.where(jnp.logical_and(plane >= 2 * K, plane < STATE), -1.0, 1.0)
    left = jnp.where(j == plane * rows + (rows - 1 - (i - plane * rows)), sign, 0.0).astype(jnp.float32)
    a = lax.broadcasted_iota(jnp.int32, (cols, cols), 0)
    b = lax.broadcasted_iota(jnp.int32, (cols, cols), 1)
    right = jnp.where(a + b == cols - 1, 1.0, 0.0).astype(jnp.float32)
    left, right = left.astype(jnp.bfloat16), right.astype(jnp.bfloat16)
    out = None
    rest = flat
    for _ in range(3):
        part = rest.astype(jnp.bfloat16)
        rest = rest - part.astype(jnp.float32)
        turned = jnp.dot(left, part, preferred_element_type=jnp.float32).astype(jnp.bfloat16)
        turned = jnp.dot(turned, right, preferred_element_type=jnp.float32)
        out = turned if out is None else out + turned
    return out.reshape(slab.shape)


def place(at, source, tiles, send_low, send_high):
    lane = lax.broadcasted_iota(jnp.int32, (8, LANES), 1)
    for group in range(PLANES // 8):
        low = jnp.zeros((8, LANES), jnp.float32)
        high = jnp.zeros((8, LANES), jnp.float32)
        for q in range(8):
            p = group * 8 + q
            lo, hi = source(p)
            here = pl.ds(PAD + at, 8)
            tiles[0][p, here] = lo
            tiles[1][p, here] = jnp.where(lane < 96, hi, lo)
            tiles[2][p, here] = jnp.where(lane < 64, shifted(lo, 32), hi)
            slot = 16 * ((q + 1) % 8)
            low = jnp.where(jnp.logical_and(lane >= 16 * q, lane < 16 * q + 16), shifted(lo, 16 * q), low)
            high = jnp.where(jnp.logical_and(lane >= slot, lane < slot + 16), shifted(hi, slot - 112), high)
        send_low[group, pl.ds(at, 8)] = low
        send_high[group, pl.ds(at, 8)] = high


def extend_kernel(x_all, m_all, w_all, tile0, tile1, tile2, send_low, send_high, cor, weights, x, m, w, sems):
    pairs = ((x_all, x), (m_all, m), (w_all, w))
    copies = [pltpu.make_async_copy(a, b, sems.at[i]) for i, (a, b) in enumerate(pairs)]
    for copy in copies:
        copy.start()
    weights[...] = line_weights()
    lat = lax.axis_index("lat")
    block = x.shape[1]
    total = block * lax.axis_size("lat")
    row = lax.broadcasted_iota(jnp.int32, cor.shape, 0) + (lat * block - HALO - PAD)
    cor[...] = jnp.sin(jnp.pi * (row.astype(jnp.float32) + 0.5) / total - jnp.pi / 2)
    for copy in copies:
        copy.wait()

    @pl.loop(0, block // 8)
    def _(g):
        r = pl.multiple_of(g * 8, 8)

        def source(p):
            if p < STATE:
                return x[p, pl.ds(r, 8), :LANES], x[p, pl.ds(r, 8), LANES:]
            if p < STATE + K:
                return m[p - STATE, pl.ds(r, 8), :LANES], m[p - STATE, pl.ds(r, 8), LANES:]
            return (
                TIMESTEP * w[pl.ds(r, 8), :LANES].astype(jnp.float32),
                TIMESTEP * w[pl.ds(r, 8), LANES:].astype(jnp.float32),
            )

        place(HALO + r, source, (tile0, tile1, tile2), send_low, send_high)


def halo_rows_kernel(ra, rb, t0, t1, t2, sl, sh, tile0, tile1, tile2, send_low, send_high, folded):
    del t0, t1, t2, sl, sh
    lat = lax.axis_index("lat")
    north_at = tile0.shape[1] - 2 * PAD - HALO

    def put(at, slab):
        for r in range(0, HALO, 8):

            def source(p, r=r):
                return slab[p, pl.ds(r, 8), :LANES], slab[p, pl.ds(r, 8), LANES:]

            place(at + r, source, (tile0, tile1, tile2), send_low, send_high)

    @pl.when(lax.rem(lat, 2) == 0)
    def _():
        put(0, ra)
        put(north_at, rb)

    @pl.when(lax.rem(lat, 2) == 1)
    def _():
        put(0, rb)

        @pl.when(lat == lax.axis_size("lat") - 1)
        def _():
            folded[...] = fold(ra[...])

        @pl.when(lat != lax.axis_size("lat") - 1)
        def _():
            folded[...] = ra[...]

        put(north_at, folded)


def extend(x, mixing, land):
    block = land.shape[0]
    span = block + 2 * HALO
    f32 = jnp.float32
    vmem = pl.BlockSpec(memory_space=pltpu.VMEM)
    tile = jax.ShapeDtypeStruct((PLANES, span + 2 * PAD, LANES), f32)
    send = jax.ShapeDtypeStruct((PLANES // 8, span, LANES), f32)
    return pl.pallas_call(
        extend_kernel,
        in_specs=[pl.BlockSpec(memory_space=pltpu.HBM)] * 3,
        out_specs=[vmem] * 7,
        out_shape=[
            tile,
            tile,
            tile,
            send,
            send,
            jax.ShapeDtypeStruct((span + 2 * PAD, LANES), f32),
            jax.ShapeDtypeStruct((2 * LANES, 4 * LANES), jnp.bfloat16),
        ],
        scratch_shapes=[
            pltpu.VMEM(x.shape, f32),
            pltpu.VMEM(mixing.shape, f32),
            pltpu.VMEM(land.shape, jnp.int32),
            pltpu.SemaphoreType.DMA((3,)),
        ],
        compiler_params=params(),
        name="extend",
    )(x, mixing, land)


def halo_rows(ra, rb, *parts):
    vmem = pl.BlockSpec(memory_space=pltpu.VMEM)
    return pl.pallas_call(
        halo_rows_kernel,
        in_specs=[vmem] * 7,
        out_specs=[vmem] * 5,
        out_shape=[jax.ShapeDtypeStruct(part.shape, part.dtype) for part in parts],
        input_output_aliases={i + 2: i for i in range(5)},
        scratch_shapes=[pltpu.VMEM(ra.shape, jnp.float32)],
        compiler_params=params(),
        name="halo_rows",
    )(ra, rb, *parts)


def line_weights():
    shape = (2 * LANES, LANES)
    here = lax.rem(lax.broadcasted_iota(jnp.int32, shape, 0), LANES)
    lane = lax.broadcasted_iota(jnp.int32, shape, 1)
    gap = lax.rem(here - lane + LANES, LANES)

    def stencil(terms):
        out = jnp.zeros(shape, jnp.float32)
        for offset, value in terms:
            out = jnp.where(gap == offset % LANES, value, out)
        return out

    east = stencil(((0, 7.0), (1, 7.0), (-1, -1.0), (2, -1.0)))
    west = stencil(((-1, 7.0), (0, 7.0), (-2, -1.0), (1, -1.0)))
    lap = stencil(((0, -4.0), (1, 1.0), (-1, 1.0)))
    diff = stencil(((1, 1.0), (-1, -1.0)))
    return jnp.concatenate([east, west, lap, diff], axis=1).astype(jnp.bfloat16)


def products(src, weights, prod, first, count):
    for f in range(4):
        planes = pl.ds(f * K, K)
        rows = pl.ds(first, count)
        q = src[planes, rows, :].reshape(K * count, LANES)
        high = q.astype(jnp.bfloat16)
        low = (q - high.astype(jnp.float32)).astype(jnp.bfloat16)
        both = jnp.concatenate([high, low], axis=1)
        got = jnp.dot(both, weights[...], preferred_element_type=jnp.float32)
        for j in range(4 if f < 3 else 3):
            prod[j, planes, rows, :] = got[:, j * LANES : (j + 1) * LANES].reshape(K, count, LANES)


def substep(src, dst, coef, cor, prod, mask, start, dst_start, span, unroll=3):
    def load(ref, p, t):
        return ref[p, pl.ds(start + t, 8, stride=span), :]

    def line(j, p, t):
        return prod[j, p, pl.ds(start + t, 8, stride=span), :]

    def density(t, k):
        return -0.25 * THERMAL * load(src, k, t) + 0.25 * HALINE * load(src, K + k, t)

    def pressures(t):
        out = [density(t, 0)]
        for k in range(1, K):
            out.append(out[-1] + density(t, k))
        return out

    def fluxes(t):
        out = [None] * STATE
        for k in range(K):
            speed = None
            for f in (3, 0, 1, 2):
                p = f * K + k
                a = load(src, p, t) + load(src, p, t + 1)
                value = 7.0 * a - (load(src, p, t - 1) + load(src, p, t + 2))
                if f == 3:
                    speed = a
                out[p] = speed * value
        return out

    def row(t, carry):
        below_flux, p_prev, p_here = carry
        wet = coef(STATE + K, t) * mask
        wet24 = wet * (1.0 / 24.0)
        wet_cor = wet * cor[pl.ds(start + t, 8, stride=span), :]
        p_next = pressures(t + 1)
        above = fluxes(t)
        grad_lon = None
        for k in range(K):
            wet_mix = wet * coef(STATE + k, t)
            drop = -0.25 * THERMAL * line(3, k, t) + 0.25 * HALINE * line(3, K + k, t)
            grad_lon = drop if k == 0 else grad_lon + drop
            u = load(src, 2 * K + k, t)
            mean = 3.0 * u + 0.5 * line(2, 2 * K + k, t)
            half = 0.5 * line(3, 2 * K + k, t)
            east_speed, west_speed = mean + half, mean - half
            for f in range(4):
                p = f * K + k
                q = load(src, p, t)
                adv = (east_speed * line(0, p, t) - west_speed * line(1, p, t)) + (above[p] - below_flux[p])
                lap = line(2, p, t) + (load(src, p, t + 1) + load(src, p, t - 1))
                if f < 2:
                    if 0 < k < K - 1:
                        lap = lap + (0.5 * (load(src, p - 1, t) + load(src, p + 1, t)) - q)
                    elif k == 0:
                        lap = lap + 0.5 * (load(src, p + 1, t) - q)
                    else:
                        lap = lap + 0.5 * (load(src, p - 1, t) - q)
                new = q + (wet_mix * lap - wet24 * adv)
                if f == 2:
                    new = new + (wet_cor * load(src, p + K, t) - wet * grad_lon)
                if f == 3:
                    new = new - (wet_cor * load(src, p - K, t) + wet * (p_next[k] - p_prev[k]))
                dst(p, pl.ds(dst_start + t, 8, stride=span), new)
        return above, p_here, p_next

    init = (fluxes(-1), pressures(-1), pressures(0))
    lax.fori_loop(0, span, row, init, unroll=unroll)


def window(tile, cor, seams, weights, prod, even, odd, out):
    span_rows = tile.shape[1] - 2 * PAD
    lane = lax.broadcasted_iota(jnp.int32, (8, LANES), 1)
    room = jnp.full((8, LANES), LANES, jnp.int32)
    for seam in seams:
        after = lax.rem(lane - seam + LANES, LANES)
        room = jnp.minimum(room, jnp.minimum(after, LANES - 1 - after))
    src = tile
    for s in range(STEPS):
        span = SPANS[s]
        need = span_rows - 4 * (s + 1)
        spare = (8 * span - need) // 2
        start = PAD + 2 * (s + 1) - spare
        keep = even if s % 2 == 0 else odd

        def put(p, rows, new, keep=keep):
            keep[p, rows, :] = new

        dst = out if s == STEPS - 1 else put
        dst_start = PAD - spare if s == STEPS - 1 else start
        lowest = PAD + 2 * (s + 1)
        first = lowest // 8 * 8
        count = -(-(lowest + need - first) // 16) * 16
        products(src, weights, prod, first, count)

        def coef(p, t, start=start, span=span):
            return tile[p, pl.ds(start + t, 8, stride=span), :]

        mask = jnp.where(room >= 2 * (s + 1), 1.0, 0.0)
        substep(src, dst, coef, cor, prod, mask, start, dst_start, span)
        src = keep


def interior_kernel(seam, tile, cor, weights, out, even, odd, prod):
    def put(p, rows, new):
        out[p, rows, :] = new

    window(tile, cor, (seam,), weights, prod, even, odd, put)


def interior(tile, cor, weights, seam):
    rows = tile.shape[1]
    block = rows - 2 * PAD - 2 * HALO
    vmem = pl.BlockSpec(memory_space=pltpu.VMEM)
    f32 = jnp.float32
    return pl.pallas_call(
        functools.partial(interior_kernel, seam),
        in_specs=[vmem] * 3,
        out_specs=vmem,
        out_shape=jax.ShapeDtypeStruct((STATE, block + 2 * PAD, LANES), f32),
        scratch_shapes=[
            pltpu.VMEM((STATE, rows, LANES), f32),
            pltpu.VMEM((STATE, rows, LANES), f32),
            pltpu.VMEM((4, STATE, rows, LANES), f32),
        ],
        compiler_params=params(),
        name="interior",
    )(tile, cor, weights)


def edge_kernel(start, cor, weights, got_low, got_high, inner0, inner1, result, tile, even, odd, prod, out_low, out_high, sems):
    span = got_low.shape[1]
    block = result.shape[1]

    @pl.loop(0, span // 8, unroll=4)
    def _(g):
        r = pl.multiple_of(g * 8, 8)
        lane = lax.broadcasted_iota(jnp.int32, (8, LANES), 1)
        for p in range(PLANES):
            q = p % 8
            mine = jnp.logical_and(lane >= 16 * q, lane < 16 * q + 16)
            both = jnp.where(mine, got_high[p // 8, pl.ds(r, 8)], got_low[p // 8, pl.ds(r, 8)])
            mid = start[p, pl.ds(PAD + r, 8)]
            tile[p, pl.ds(PAD + r, 8)] = jnp.where(lane < 32, shifted(both, -16 * q), mid)

    def put(p, rows, new):
        lane = lax.broadcasted_iota(jnp.int32, (8, LANES), 1)
        lo = inner0[p, rows, :]
        hi = inner1[p, rows, :]
        out_low[p, rows, :] = jnp.where(lane < 16, shifted(new, -32), jnp.where(lane < 112, lo, hi))
        out_high[p, rows, :] = jnp.where(lane < 80, hi, new)

    window(tile, cor, (16, 64), weights, prod, even, odd, put)
    copies = []
    for i, half in enumerate((out_low, out_high)):
        source = half.at[:, pl.ds(PAD, block), :]
        copies.append(pltpu.make_async_copy(source, result.at[:, :, pl.ds(i * LANES, LANES)], sems.at[i]))
    for copy in copies:
        copy.start()
    for copy in copies:
        copy.wait()


def edges(start, cor, weights, got_low, got_high, inner0, inner1):
    rows = start.shape[1]
    block = rows - 2 * PAD - 2 * HALO
    f32 = jnp.float32
    vmem = pl.BlockSpec(memory_space=pltpu.VMEM)
    return pl.pallas_call(
        edge_kernel,
        in_specs=[vmem] * 7,
        out_specs=pl.BlockSpec(memory_space=pltpu.HBM),
        out_shape=jax.ShapeDtypeStruct((STATE, block, 2 * LANES), f32),
        scratch_shapes=[
            pltpu.VMEM((PLANES, rows, LANES), f32),
            pltpu.VMEM((STATE, rows, LANES), f32),
            pltpu.VMEM((STATE, rows, LANES), f32),
            pltpu.VMEM((4, STATE, rows, LANES), f32),
            pltpu.VMEM((STATE, block + 2 * PAD, LANES), f32),
            pltpu.VMEM((STATE, block + 2 * PAD, LANES), f32),
            pltpu.SemaphoreType.DMA((2,)),
        ],
        compiler_params=params(),
        name="edges",
    )(start, cor, weights, got_low, got_high, inner0, inner1)


def body(ocean_state, mixing, land_sea):
    block, cols = land_sea.shape
    n_lon, n_lat = lax.axis_size("lon"), lax.axis_size("lat")
    axes = ("lon", "lat")

    def at(i, l):
        return (i % n_lon) * n_lat + l

    pairs_b = [(at(i, l), at(i, l ^ 1)) for i in range(n_lon) for l in range(n_lat)]
    pairs_a = []
    for i in range(n_lon):
        for l in range(1, n_lat - 1, 2):
            pairs_a += [(at(i, l), at(i, l + 1)), (at(i, l + 1), at(i, l))]
        pairs_a.append((at(i, n_lat - 1), at(n_lon - 1 - i, n_lat - 1)))
    east = [(i, (i + 1) % n_lon) for i in range(n_lon)]
    west = [((i + 1) % n_lon, i) for i in range(n_lon)]

    x = ocean_state.reshape(STATE, block, cols)
    x, mixing, land_sea = (pltpu.with_memory_space_constraint(v, pltpu.HBM) for v in (x, mixing, land_sea))
    to_a, to_b = pack_rows(x, mixing, land_sea)
    ra = lax.ppermute(to_a, axes, pairs_a)
    rb = lax.ppermute(to_b, axes, pairs_b)
    *parts, cor, weights = extend(x, mixing, land_sea)
    tile0, tile1, tile2, send_low, send_high = halo_rows(ra, rb, *parts)
    inner0 = interior(tile0, cor, weights, 0)
    send_low, send_high, inner0 = lax.optimization_barrier((send_low, send_high, inner0))
    got_low = lax.ppermute(send_high, "lon", east)
    got_high = lax.ppermute(send_low, "lon", west)
    inner1 = interior(tile1, cor, weights, 96)
    out = edges(tile2, cor, weights, got_low, got_high, inner0, inner1)
    return out.reshape(ocean_state.shape)


def solution(mesh):
    in_specs = (P(None, None, "lat", "lon"), P(None, "lat", "lon"), P("lat", "lon"))
    out_specs = P(None, None, "lat", "lon")
    return jax.shard_map(body, mesh=mesh, in_specs=in_specs, out_specs=out_specs, check_vma=False)
```

```python
import functools
import jax
import jax.numpy as jnp
from jax import lax
from jax.experimental import pallas as pl
from jax.experimental.pallas import tpu as pltpu
from jax.sharding import PartitionSpec as P

STEPS = 8
K = 3
HALO = 2 * STEPS
LANES = 128
PAD = 8

THERMAL = 0.2
HALINE = 0.15
GRAVITY = 0.5
TIMESTEP = 0.1

STATE = 4 * K
PLANES = STATE + K + 1
VMEM_LIMIT = 24 * 1024 * 1024
CORE_SPAN = 17
SPANS = (21, 19, 19, 19, 19, 17, 17, 17)


def params():
    return pltpu.CompilerParams(vmem_limit_bytes=VMEM_LIMIT)


def shifted(x, by):
    return pltpu.roll(x, by % LANES, 1)


def pack_rows_kernel(x, m, w, to_a, to_b, wet, sems):
    even = lax.rem(lax.axis_index("lat"), 2) == 0
    last = x.shape[1] - HALO
    starts = (jnp.where(even, 0, last), jnp.where(even, last, 0))
    copies = []
    for i, dest in enumerate((to_a, to_b)):
        rows = pl.ds(pl.multiple_of(starts[i], HALO), HALO)
        copies.append(pltpu.make_async_copy(x.at[:, rows, :], dest.at[pl.ds(0, STATE)], sems.at[3 * i]))
        copies.append(pltpu.make_async_copy(m.at[:, rows, :], dest.at[pl.ds(STATE, K)], sems.at[3 * i + 1]))
        copies.append(pltpu.make_async_copy(w.at[rows, :], wet.at[i], sems.at[3 * i + 2]))
    for copy in copies:
        copy.start()
    for copy in copies:
        copy.wait()
    for i, dest in enumerate((to_a, to_b)):
        dest[STATE + K] = TIMESTEP * wet[i].astype(jnp.float32)


def pack_rows(x, mixing, land):
    cols = land.shape[1]
    slab = jax.ShapeDtypeStruct((PLANES, HALO, cols), jnp.float32)
    return pl.pallas_call(
        pack_rows_kernel,
        in_specs=[pl.BlockSpec(memory_space=pltpu.HBM)] * 3,
        out_specs=[pl.BlockSpec(memory_space=pltpu.VMEM)] * 2,
        out_shape=[slab, slab],
        scratch_shapes=[pltpu.VMEM((2, HALO, cols), jnp.int32), pltpu.SemaphoreType.DMA((6,))],
        compiler_params=params(),
        name="pack_rows",
    )(x, mixing, land)


def fold(slab):
    planes, rows, cols = slab.shape
    flat = slab.reshape(planes * rows, cols)
    n = planes * rows
    i = lax.broadcasted_iota(jnp.int32, (n, n), 0)
    j = lax.broadcasted_iota(jnp.int32, (n, n), 1)
    plane = i // rows
    sign = jnp.where(jnp.logical_and(plane >= 2 * K, plane < STATE), -1.0, 1.0)
    left = jnp.where(j == plane * rows + (rows - 1 - (i - plane * rows)), sign, 0.0).astype(jnp.float32)
    a = lax.broadcasted_iota(jnp.int32, (cols, cols), 0)
    b = lax.broadcasted_iota(jnp.int32, (cols, cols), 1)
    right = jnp.where(a + b == cols - 1, 1.0, 0.0).astype(jnp.float32)
    left, right = left.astype(jnp.bfloat16), right.astype(jnp.bfloat16)
    out = None
    rest = flat
    for _ in range(3):
        part = rest.astype(jnp.bfloat16)
        rest = rest - part.astype(jnp.float32)
        turned = jnp.dot(left, part, preferred_element_type=jnp.float32).astype(jnp.bfloat16)
        turned = jnp.dot(turned, right, preferred_element_type=jnp.float32)
        out = turned if out is None else out + turned
    return out.reshape(slab.shape)


def place(at, source, tiles, send_low, send_high):
    lane = lax.broadcasted_iota(jnp.int32, (8, LANES), 1)
    for group in range(PLANES // 8):
        low = jnp.zeros((8, LANES), jnp.float32)
        high = jnp.zeros((8, LANES), jnp.float32)
        for q in range(8):
            p = group * 8 + q
            lo, hi = source(p)
            here = pl.ds(PAD + at, 8)
            tiles[0][p, here] = lo
            tiles[1][p, here] = jnp.where(lane < 96, hi, lo)
            tiles[2][p, here] = jnp.where(lane < 64, shifted(lo, 32), hi)
            slot = 16 * ((q + 1) % 8)
            low = jnp.where(jnp.logical_and(lane >= 16 * q, lane < 16 * q + 16), shifted(lo, 16 * q), low)
            high = jnp.where(jnp.logical_and(lane >= slot, lane < slot + 16), shifted(hi, slot - 112), high)
        send_low[group, pl.ds(at, 8)] = low
        send_high[group, pl.ds(at, 8)] = high


def extend_kernel(x_all, m_all, w_all, tile0, tile1, tile2, send_low, send_high, cor, weights, even0, even1, x, m, w, prod, sems):
    pairs = ((x_all, x), (m_all, m), (w_all, w))
    copies = [pltpu.make_async_copy(a, b, sems.at[i]) for i, (a, b) in enumerate(pairs)]
    for copy in copies:
        copy.start()
    weights[...] = line_weights()
    lat = lax.axis_index("lat")
    block = x.shape[1]
    total = block * lax.axis_size("lat")
    row = lax.broadcasted_iota(jnp.int32, cor.shape, 0) + (lat * block - HALO - PAD)
    cor[...] = jnp.sin(jnp.pi * (row.astype(jnp.float32) + 0.5) / total - jnp.pi / 2)
    for copy in copies:
        copy.wait()

    @pl.loop(0, block // 8)
    def _(g):
        r = pl.multiple_of(g * 8, 8)

        def source(p):
            if p < STATE:
                return x[p, pl.ds(r, 8), :LANES], x[p, pl.ds(r, 8), LANES:]
            if p < STATE + K:
                return m[p - STATE, pl.ds(r, 8), :LANES], m[p - STATE, pl.ds(r, 8), LANES:]
            return (
                TIMESTEP * w[pl.ds(r, 8), :LANES].astype(jnp.float32),
                TIMESTEP * w[pl.ds(r, 8), LANES:].astype(jnp.float32),
            )

        place(HALO + r, source, (tile0, tile1, tile2), send_low, send_high)

    early(tile0, cor, (0,), weights, prod, even0)
    early(tile1, cor, (96,), weights, prod, even1)


def halo_rows_kernel(ra, rb, t0, t1, t2, sl, sh, tile0, tile1, tile2, send_low, send_high, folded):
    del t0, t1, t2, sl, sh
    lat = lax.axis_index("lat")
    north_at = tile0.shape[1] - 2 * PAD - HALO

    def put(at, slab):
        for r in range(0, HALO, 8):

            def source(p, r=r):
                return slab[p, pl.ds(r, 8), :LANES], slab[p, pl.ds(r, 8), LANES:]

            place(at + r, source, (tile0, tile1, tile2), send_low, send_high)

    @pl.when(lax.rem(lat, 2) == 0)
    def _():
        put(0, ra)
        put(north_at, rb)

    @pl.when(lax.rem(lat, 2) == 1)
    def _():
        put(0, rb)

        @pl.when(lat == lax.axis_size("lat") - 1)
        def _():
            folded[...] = fold(ra[...])

        @pl.when(lat != lax.axis_size("lat") - 1)
        def _():
            folded[...] = ra[...]

        put(north_at, folded)


def extend(x, mixing, land):
    block = land.shape[0]
    span = block + 2 * HALO
    f32 = jnp.float32
    vmem = pl.BlockSpec(memory_space=pltpu.VMEM)
    tile = jax.ShapeDtypeStruct((PLANES, span + 2 * PAD, LANES), f32)
    send = jax.ShapeDtypeStruct((PLANES // 8, span, LANES), f32)
    even = jax.ShapeDtypeStruct((STATE, span + 2 * PAD, LANES), f32)
    return pl.pallas_call(
        extend_kernel,
        in_specs=[pl.BlockSpec(memory_space=pltpu.HBM)] * 3,
        out_specs=[vmem] * 9,
        out_shape=[
            tile,
            tile,
            tile,
            send,
            send,
            jax.ShapeDtypeStruct((span + 2 * PAD, LANES), f32),
            jax.ShapeDtypeStruct((2 * LANES, 4 * LANES), jnp.bfloat16),
            even,
            even,
        ],
        scratch_shapes=[
            pltpu.VMEM(x.shape, f32),
            pltpu.VMEM(mixing.shape, f32),
            pltpu.VMEM(land.shape, jnp.int32),
            pltpu.VMEM((4,) + even.shape, f32),
            pltpu.SemaphoreType.DMA((3,)),
        ],
        compiler_params=params(),
        name="extend",
    )(x, mixing, land)


def halo_rows(ra, rb, *parts):
    vmem = pl.BlockSpec(memory_space=pltpu.VMEM)
    return pl.pallas_call(
        halo_rows_kernel,
        in_specs=[vmem] * 7,
        out_specs=[vmem] * 5,
        out_shape=[jax.ShapeDtypeStruct(part.shape, part.dtype) for part in parts],
        input_output_aliases={i + 2: i for i in range(5)},
        scratch_shapes=[pltpu.VMEM(ra.shape, jnp.float32)],
        compiler_params=params(),
        name="halo_rows",
    )(ra, rb, *parts)


def line_weights():
    shape = (2 * LANES, LANES)
    here = lax.rem(lax.broadcasted_iota(jnp.int32, shape, 0), LANES)
    lane = lax.broadcasted_iota(jnp.int32, shape, 1)
    gap = lax.rem(here - lane + LANES, LANES)

    def stencil(terms):
        out = jnp.zeros(shape, jnp.float32)
        for offset, value in terms:
            out = jnp.where(gap == offset % LANES, value, out)
        return out

    east = stencil(((0, 7.0), (1, 7.0), (-1, -1.0), (2, -1.0)))
    west = stencil(((-1, 7.0), (0, 7.0), (-2, -1.0), (1, -1.0)))
    lap = stencil(((0, -4.0), (1, 1.0), (-1, 1.0)))
    diff = stencil(((1, 1.0), (-1, -1.0)))
    return jnp.concatenate([east, west, lap, diff], axis=1).astype(jnp.bfloat16)


def products(src, weights, prod, first, count):
    for f in range(4):
        planes = pl.ds(f * K, K)
        rows = pl.ds(first, count)
        q = src[planes, rows, :].reshape(K * count, LANES)
        high = q.astype(jnp.bfloat16)
        low = (q - high.astype(jnp.float32)).astype(jnp.bfloat16)
        both = jnp.concatenate([high, low], axis=1)
        got = jnp.dot(both, weights[...], preferred_element_type=jnp.float32)
        for j in range(4 if f < 3 else 3):
            prod[j, planes, rows, :] = got[:, j * LANES : (j + 1) * LANES].reshape(K, count, LANES)


def tail_products(src, weights, prod, firsts, count):
    q = jnp.concatenate([src[pl.ds(0, STATE), pl.ds(f, count), :].reshape(STATE * count, LANES) for f in firsts], axis=0)
    high = q.astype(jnp.bfloat16)
    low = (q - high.astype(jnp.float32)).astype(jnp.bfloat16)
    got = jnp.dot(jnp.concatenate([high, low], axis=1), weights[...], preferred_element_type=jnp.float32)
    n = STATE * count
    for i, f in enumerate(firsts):
        for j in range(4):
            part = got[i * n : (i + 1) * n, j * LANES : (j + 1) * LANES]
            prod[j, pl.ds(0, STATE), pl.ds(f, count), :] = part.reshape(STATE, count, LANES)


def seam_room(seams):
    lane = lax.broadcasted_iota(jnp.int32, (8, LANES), 1)
    room = jnp.full((8, LANES), LANES, jnp.int32)
    for seam in seams:
        after = lax.rem(lane - seam + LANES, LANES)
        room = jnp.minimum(room, jnp.minimum(after, LANES - 1 - after))
    return room


def first_substep(tile, cor, seams, weights, prod, even, pieces):
    mask = jnp.where(seam_room(seams) >= 2, 1.0, 0.0)

    def put(p, rows, new):
        even[p, rows, :] = new

    for start, span in pieces:

        def coef(p, t, start=start, span=span):
            return tile[p, pl.ds(start + t, 8, stride=span), :]

        substep(tile, put, coef, cor, prod, mask, start, start, span)


def early(tile, cor, seams, weights, prod, even):
    first = PAD + HALO
    block = tile.shape[1] - 2 * first
    products(tile, weights, prod, first, block)
    spare = (8 * CORE_SPAN - (block - 4)) // 2
    first_substep(tile, cor, seams, weights, prod, even, [(first + 2 - spare, CORE_SPAN)])


def late(tile, cor, seams, weights, prod, even):
    south = PAD + 2
    north = tile.shape[1] - south - HALO
    tail_products(tile, weights, prod, (south // 8 * 8, north // 8 * 8), HALO + 8)
    first_substep(tile, cor, seams, weights, prod, even, [(south, 2), (north, 2)])


def substep(src, dst, coef, cor, prod, mask, start, dst_start, span, unroll=3):
    def load(ref, p, t):
        return ref[p, pl.ds(start + t, 8, stride=span), :]

    def line(j, p, t):
        return prod[j, p, pl.ds(start + t, 8, stride=span), :]

    def density(t, k):
        return -0.25 * THERMAL * load(src, k, t) + 0.25 * HALINE * load(src, K + k, t)

    def pressures(t):
        out = [density(t, 0)]
        for k in range(1, K):
            out.append(out[-1] + density(t, k))
        return out

    def fluxes(t):
        out = [None] * STATE
        for k in range(K):
            speed = None
            for f in (3, 0, 1, 2):
                p = f * K + k
                a = load(src, p, t) + load(src, p, t + 1)
                value = 7.0 * a - (load(src, p, t - 1) + load(src, p, t + 2))
                if f == 3:
                    speed = a
                out[p] = speed * value
        return out

    def row(t, carry):
        below_flux, p_prev, p_here = carry
        wet = coef(STATE + K, t) * mask
        wet24 = wet * (1.0 / 24.0)
        wet_cor = wet * cor[pl.ds(start + t, 8, stride=span), :]
        p_next = pressures(t + 1)
        above = fluxes(t)
        grad_lon = None
        for k in range(K):
            wet_mix = wet * coef(STATE + k, t)
            drop = -0.25 * THERMAL * line(3, k, t) + 0.25 * HALINE * line(3, K + k, t)
            grad_lon = drop if k == 0 else grad_lon + drop
            u = load(src, 2 * K + k, t)
            mean = 3.0 * u + 0.5 * line(2, 2 * K + k, t)
            half = 0.5 * line(3, 2 * K + k, t)
            east_speed, west_speed = mean + half, mean - half
            for f in range(4):
                p = f * K + k
                q = load(src, p, t)
                adv = (east_speed * line(0, p, t) - west_speed * line(1, p, t)) + (above[p] - below_flux[p])
                lap = line(2, p, t) + (load(src, p, t + 1) + load(src, p, t - 1))
                if f < 2:
                    if 0 < k < K - 1:
                        lap = lap + (0.5 * (load(src, p - 1, t) + load(src, p + 1, t)) - q)
                    elif k == 0:
                        lap = lap + 0.5 * (load(src, p + 1, t) - q)
                    else:
                        lap = lap + 0.5 * (load(src, p - 1, t) - q)
                new = q + (wet_mix * lap - wet24 * adv)
                if f == 2:
                    new = new + (wet_cor * load(src, p + K, t) - wet * grad_lon)
                if f == 3:
                    new = new - (wet_cor * load(src, p - K, t) + wet * (p_next[k] - p_prev[k]))
                dst(p, pl.ds(dst_start + t, 8, stride=span), new)
        return above, p_here, p_next

    init = (fluxes(-1), pressures(-1), pressures(0))
    lax.fori_loop(0, span, row, init, unroll=unroll)


def window(tile, cor, seams, weights, prod, even, odd, out, started=False):
    span_rows = tile.shape[1] - 2 * PAD
    room = seam_room(seams)
    src = tile
    for s in range(STEPS):
        if s == 0 and started:
            late(tile, cor, seams, weights, prod, even)
            src = even
            continue
        span = SPANS[s]
        need = span_rows - 4 * (s + 1)
        spare = (8 * span - need) // 2
        start = PAD + 2 * (s + 1) - spare
        keep = even if s % 2 == 0 else odd

        def put(p, rows, new, keep=keep):
            keep[p, rows, :] = new

        dst = out if s == STEPS - 1 else put
        dst_start = PAD - spare if s == STEPS - 1 else start
        lowest = PAD + 2 * (s + 1)
        first = lowest // 8 * 8
        count = -(-(lowest + need - first) // 16) * 16
        products(src, weights, prod, first, count)

        def coef(p, t, start=start, span=span):
            return tile[p, pl.ds(start + t, 8, stride=span), :]

        mask = jnp.where(room >= 2 * (s + 1), 1.0, 0.0)
        substep(src, dst, coef, cor, prod, mask, start, dst_start, span)
        src = keep


def interior_kernel(seam, tile, cor, weights, begun, out, even, odd, prod):
    del begun

    def put(p, rows, new):
        out[p, rows, :] = new

    window(tile, cor, (seam,), weights, prod, even, odd, put, started=True)


def interior(tile, cor, weights, begun, seam):
    rows = tile.shape[1]
    block = rows - 2 * PAD - 2 * HALO
    vmem = pl.BlockSpec(memory_space=pltpu.VMEM)
    f32 = jnp.float32
    return pl.pallas_call(
        functools.partial(interior_kernel, seam),
        in_specs=[vmem] * 4,
        out_specs=[vmem, vmem],
        out_shape=[
            jax.ShapeDtypeStruct((STATE, block + 2 * PAD, LANES), f32),
            jax.ShapeDtypeStruct(begun.shape, f32),
        ],
        input_output_aliases={3: 1},
        scratch_shapes=[
            pltpu.VMEM((STATE, rows, LANES), f32),
            pltpu.VMEM((4, STATE, rows, LANES), f32),
        ],
        compiler_params=params(),
        name="interior",
    )(tile, cor, weights, begun)[0]


def edge_kernel(start, cor, weights, got_low, got_high, inner0, inner1, result, tile, even, odd, prod, out_low, out_high, sems):
    span = got_low.shape[1]
    block = result.shape[1]

    @pl.loop(0, span // 8, unroll=4)
    def _(g):
        r = pl.multiple_of(g * 8, 8)
        lane = lax.broadcasted_iota(jnp.int32, (8, LANES), 1)
        for p in range(PLANES):
            q = p % 8
            mine = jnp.logical_and(lane >= 16 * q, lane < 16 * q + 16)
            both = jnp.where(mine, got_high[p // 8, pl.ds(r, 8)], got_low[p // 8, pl.ds(r, 8)])
            mid = start[p, pl.ds(PAD + r, 8)]
            tile[p, pl.ds(PAD + r, 8)] = jnp.where(lane < 32, shifted(both, -16 * q), mid)

    def put(p, rows, new):
        lane = lax.broadcasted_iota(jnp.int32, (8, LANES), 1)
        lo = inner0[p, rows, :]
        hi = inner1[p, rows, :]
        out_low[p, rows, :] = jnp.where(lane < 16, shifted(new, -32), jnp.where(lane < 112, lo, hi))
        out_high[p, rows, :] = jnp.where(lane < 80, hi, new)

    window(tile, cor, (16, 64), weights, prod, even, odd, put)
    copies = []
    for i, half in enumerate((out_low, out_high)):
        source = half.at[:, pl.ds(PAD, block), :]
        copies.append(pltpu.make_async_copy(source, result.at[:, :, pl.ds(i * LANES, LANES)], sems.at[i]))
    for copy in copies:
        copy.start()
    for copy in copies:
        copy.wait()


def edges(start, cor, weights, got_low, got_high, inner0, inner1):
    rows = start.shape[1]
    block = rows - 2 * PAD - 2 * HALO
    f32 = jnp.float32
    vmem = pl.BlockSpec(memory_space=pltpu.VMEM)
    return pl.pallas_call(
        edge_kernel,
        in_specs=[vmem] * 7,
        out_specs=pl.BlockSpec(memory_space=pltpu.HBM),
        out_shape=jax.ShapeDtypeStruct((STATE, block, 2 * LANES), f32),
        scratch_shapes=[
            pltpu.VMEM((PLANES, rows, LANES), f32),
            pltpu.VMEM((STATE, rows, LANES), f32),
            pltpu.VMEM((STATE, rows, LANES), f32),
            pltpu.VMEM((4, STATE, rows, LANES), f32),
            pltpu.VMEM((STATE, block + 2 * PAD, LANES), f32),
            pltpu.VMEM((STATE, block + 2 * PAD, LANES), f32),
            pltpu.SemaphoreType.DMA((2,)),
        ],
        compiler_params=params(),
        name="edges",
    )(start, cor, weights, got_low, got_high, inner0, inner1)


def body(ocean_state, mixing, land_sea):
    block, cols = land_sea.shape
    n_lon, n_lat = lax.axis_size("lon"), lax.axis_size("lat")
    axes = ("lon", "lat")

    def at(i, l):
        return (i % n_lon) * n_lat + l

    pairs_b = [(at(i, l), at(i, l ^ 1)) for i in range(n_lon) for l in range(n_lat)]
    pairs_a = []
    for i in range(n_lon):
        for l in range(1, n_lat - 1, 2):
            pairs_a += [(at(i, l), at(i, l + 1)), (at(i, l + 1), at(i, l))]
        pairs_a.append((at(i, n_lat - 1), at(n_lon - 1 - i, n_lat - 1)))
    east = [(i, (i + 1) % n_lon) for i in range(n_lon)]
    west = [((i + 1) % n_lon, i) for i in range(n_lon)]

    x = ocean_state.reshape(STATE, block, cols)
    x, mixing, land_sea = (pltpu.with_memory_space_constraint(v, pltpu.HBM) for v in (x, mixing, land_sea))
    to_a, to_b = pack_rows(x, mixing, land_sea)
    ra = lax.ppermute(to_a, axes, pairs_a)
    rb = lax.ppermute(to_b, axes, pairs_b)
    *parts, cor, weights, even0, even1 = extend(x, mixing, land_sea)
    tile0, tile1, tile2, send_low, send_high = halo_rows(ra, rb, *parts)
    inner0 = interior(tile0, cor, weights, even0, 0)
    send_low, send_high, inner0 = lax.optimization_barrier((send_low, send_high, inner0))
    got_low = lax.ppermute(send_high, "lon", east)
    got_high = lax.ppermute(send_low, "lon", west)
    inner1 = interior(tile1, cor, weights, even1, 96)
    out = edges(tile2, cor, weights, got_low, got_high, inner0, inner1)
    return out.reshape(ocean_state.shape)


def solution(mesh):
    in_specs = (P(None, None, "lat", "lon"), P(None, "lat", "lon"), P("lat", "lon"))
    out_specs = P(None, None, "lat", "lon")
    return jax.shard_map(body, mesh=mesh, in_specs=in_specs, out_specs=out_specs, check_vma=False)
```

```python
import functools
import jax
import jax.numpy as jnp
from jax import lax
from jax.experimental import pallas as pl
from jax.experimental.pallas import tpu as pltpu
from jax.sharding import PartitionSpec as P

STEPS = 8
K = 3
HALO = 2 * STEPS
LANES = 128
PAD = 8

THERMAL = 0.2
HALINE = 0.15
GRAVITY = 0.5
TIMESTEP = 0.1

STATE = 4 * K
PLANES = STATE + K + 1
VMEM_LIMIT = 24 * 1024 * 1024
SPANS = (21, 19, 19, 19, 19, 17, 17, 17)


def params():
    return pltpu.CompilerParams(vmem_limit_bytes=VMEM_LIMIT)


def shifted(x, by):
    return pltpu.roll(x, by % LANES, 1)


def pack_rows_kernel(x, m, w, to_a, to_b, wet, sems):
    even = lax.rem(lax.axis_index("lat"), 2) == 0
    last = x.shape[1] - HALO
    starts = (jnp.where(even, 0, last), jnp.where(even, last, 0))
    copies = []
    for i, dest in enumerate((to_a, to_b)):
        rows = pl.ds(pl.multiple_of(starts[i], HALO), HALO)
        copies.append(pltpu.make_async_copy(x.at[:, rows, :], dest.at[pl.ds(0, STATE)], sems.at[3 * i]))
        copies.append(pltpu.make_async_copy(m.at[:, rows, :], dest.at[pl.ds(STATE, K)], sems.at[3 * i + 1]))
        copies.append(pltpu.make_async_copy(w.at[rows, :], wet.at[i], sems.at[3 * i + 2]))
    for copy in copies:
        copy.start()
    for copy in copies:
        copy.wait()
    for i, dest in enumerate((to_a, to_b)):
        dest[STATE + K] = TIMESTEP * wet[i].astype(jnp.float32)


def pack_rows(x, mixing, land):
    cols = land.shape[1]
    slab = jax.ShapeDtypeStruct((PLANES, HALO, cols), jnp.float32)
    return pl.pallas_call(
        pack_rows_kernel,
        in_specs=[pl.BlockSpec(memory_space=pltpu.HBM)] * 3,
        out_specs=[pl.BlockSpec(memory_space=pltpu.VMEM)] * 2,
        out_shape=[slab, slab],
        scratch_shapes=[pltpu.VMEM((2, HALO, cols), jnp.int32), pltpu.SemaphoreType.DMA((6,))],
        compiler_params=params(),
        name="pack_rows",
    )(x, mixing, land)


def fold(slab):
    planes, rows, cols = slab.shape
    flat = slab.reshape(planes * rows, cols)
    n = planes * rows
    i = lax.broadcasted_iota(jnp.int32, (n, n), 0)
    j = lax.broadcasted_iota(jnp.int32, (n, n), 1)
    plane = i // rows
    sign = jnp.where(jnp.logical_and(plane >= 2 * K, plane < STATE), -1.0, 1.0)
    left = jnp.where(j == plane * rows + (rows - 1 - (i - plane * rows)), sign, 0.0).astype(jnp.float32)
    a = lax.broadcasted_iota(jnp.int32, (cols, cols), 0)
    b = lax.broadcasted_iota(jnp.int32, (cols, cols), 1)
    right = jnp.where(a + b == cols - 1, 1.0, 0.0).astype(jnp.float32)
    left, right = left.astype(jnp.bfloat16), right.astype(jnp.bfloat16)
    out = None
    rest = flat
    for _ in range(3):
        part = rest.astype(jnp.bfloat16)
        rest = rest - part.astype(jnp.float32)
        turned = jnp.dot(left, part, preferred_element_type=jnp.float32).astype(jnp.bfloat16)
        turned = jnp.dot(turned, right, preferred_element_type=jnp.float32)
        out = turned if out is None else out + turned
    return out.reshape(slab.shape)


def place(at, source, tiles, send_low, send_high):
    lane = lax.broadcasted_iota(jnp.int32, (8, LANES), 1)
    for group in range(PLANES // 8):
        low = jnp.zeros((8, LANES), jnp.float32)
        high = jnp.zeros((8, LANES), jnp.float32)
        for q in range(8):
            p = group * 8 + q
            lo, hi = source(p)
            here = pl.ds(PAD + at, 8)
            tiles[0][p, here] = lo
            tiles[1][p, here] = jnp.where(lane < 96, hi, lo)
            tiles[2][p, here] = jnp.where(lane < 64, shifted(lo, 32), hi)
            slot = 16 * ((q + 1) % 8)
            low = jnp.where(jnp.logical_and(lane >= 16 * q, lane < 16 * q + 16), shifted(lo, 16 * q), low)
            high = jnp.where(jnp.logical_and(lane >= slot, lane < slot + 16), shifted(hi, slot - 112), high)
        send_low[group, pl.ds(at, 8)] = low
        send_high[group, pl.ds(at, 8)] = high


def extend_kernel(x_all, m_all, w_all, tile0, tile1, tile2, send_low, send_high, cor, weights, x, m, w, sems):
    pairs = ((x_all, x), (m_all, m), (w_all, w))
    copies = [pltpu.make_async_copy(a, b, sems.at[i]) for i, (a, b) in enumerate(pairs)]
    for copy in copies:
        copy.start()
    weights[...] = line_weights()
    lat = lax.axis_index("lat")
    block = x.shape[1]
    total = block * lax.axis_size("lat")
    row = lax.broadcasted_iota(jnp.int32, cor.shape, 0) + (lat * block - HALO - PAD)
    cor[...] = jnp.sin(jnp.pi * (row.astype(jnp.float32) + 0.5) / total - jnp.pi / 2)
    for copy in copies:
        copy.wait()

    @pl.loop(0, block // 8)
    def _(g):
        r = pl.multiple_of(g * 8, 8)

        def source(p):
            if p < STATE:
                return x[p, pl.ds(r, 8), :LANES], x[p, pl.ds(r, 8), LANES:]
            if p < STATE + K:
                return m[p - STATE, pl.ds(r, 8), :LANES], m[p - STATE, pl.ds(r, 8), LANES:]
            return (
                TIMESTEP * w[pl.ds(r, 8), :LANES].astype(jnp.float32),
                TIMESTEP * w[pl.ds(r, 8), LANES:].astype(jnp.float32),
            )

        place(HALO + r, source, (tile0, tile1, tile2), send_low, send_high)


def halo_rows_kernel(ra, rb, t0, t1, t2, sl, sh, tile0, tile1, tile2, send_low, send_high, folded):
    del t0, t1, t2, sl, sh
    lat = lax.axis_index("lat")
    north_at = tile0.shape[1] - 2 * PAD - HALO

    def put(at, slab):
        for r in range(0, HALO, 8):

            def source(p, r=r):
                return slab[p, pl.ds(r, 8), :LANES], slab[p, pl.ds(r, 8), LANES:]

            place(at + r, source, (tile0, tile1, tile2), send_low, send_high)

    @pl.when(lax.rem(lat, 2) == 0)
    def _():
        put(0, ra)
        put(north_at, rb)

    @pl.when(lax.rem(lat, 2) == 1)
    def _():
        put(0, rb)

        @pl.when(lat == lax.axis_size("lat") - 1)
        def _():
            folded[...] = fold(ra[...])

        @pl.when(lat != lax.axis_size("lat") - 1)
        def _():
            folded[...] = ra[...]

        put(north_at, folded)


def extend(x, mixing, land):
    block = land.shape[0]
    span = block + 2 * HALO
    f32 = jnp.float32
    vmem = pl.BlockSpec(memory_space=pltpu.VMEM)
    tile = jax.ShapeDtypeStruct((PLANES, span + 2 * PAD, LANES), f32)
    send = jax.ShapeDtypeStruct((PLANES // 8, span, LANES), f32)
    return pl.pallas_call(
        extend_kernel,
        in_specs=[pl.BlockSpec(memory_space=pltpu.HBM)] * 3,
        out_specs=[vmem] * 7,
        out_shape=[
            tile,
            tile,
            tile,
            send,
            send,
            jax.ShapeDtypeStruct((span + 2 * PAD, LANES), f32),
            jax.ShapeDtypeStruct((2 * LANES, 4 * LANES), jnp.bfloat16),
        ],
        scratch_shapes=[
            pltpu.VMEM(x.shape, f32),
            pltpu.VMEM(mixing.shape, f32),
            pltpu.VMEM(land.shape, jnp.int32),
            pltpu.SemaphoreType.DMA((3,)),
        ],
        compiler_params=params(),
        name="extend",
    )(x, mixing, land)


def halo_rows(ra, rb, *parts):
    vmem = pl.BlockSpec(memory_space=pltpu.VMEM)
    return pl.pallas_call(
        halo_rows_kernel,
        in_specs=[vmem] * 7,
        out_specs=[vmem] * 5,
        out_shape=[jax.ShapeDtypeStruct(part.shape, part.dtype) for part in parts],
        input_output_aliases={i + 2: i for i in range(5)},
        scratch_shapes=[pltpu.VMEM(ra.shape, jnp.float32)],
        compiler_params=params(),
        name="halo_rows",
    )(ra, rb, *parts)


def line_weights():
    shape = (2 * LANES, LANES)
    here = lax.rem(lax.broadcasted_iota(jnp.int32, shape, 0), LANES)
    lane = lax.broadcasted_iota(jnp.int32, shape, 1)
    gap = lax.rem(here - lane + LANES, LANES)

    def stencil(terms):
        out = jnp.zeros(shape, jnp.float32)
        for offset, value in terms:
            out = jnp.where(gap == offset % LANES, value, out)
        return out

    east = stencil(((0, 3.5), (1, 3.5), (-1, -0.5), (2, -0.5)))
    west = stencil(((-1, 3.5), (0, 3.5), (-2, -0.5), (1, -0.5)))
    lap = stencil(((0, -4.0), (1, 1.0), (-1, 1.0)))
    diff = stencil(((1, 1.0), (-1, -1.0)))
    return jnp.concatenate([east, west, lap, diff], axis=1).astype(jnp.bfloat16)


def products(src, weights, prod, first, count):
    for f in range(4):
        planes = pl.ds(f * K, K)
        rows = pl.ds(first, count)
        q = src[planes, rows, :].reshape(K * count, LANES)
        high = q.astype(jnp.bfloat16)
        low = (q - high.astype(jnp.float32)).astype(jnp.bfloat16)
        both = jnp.concatenate([high, low], axis=1)
        got = jnp.dot(both, weights[...], preferred_element_type=jnp.float32)
        for j in range(4 if f < 3 else 3):
            prod[j, planes, rows, :] = got[:, j * LANES : (j + 1) * LANES].reshape(K, count, LANES)


def substep(src, dst, coef, cor, prod, mask, start, dst_start, span, unroll=4):
    def load(ref, p, t):
        return ref[p, pl.ds(start + t, 8, stride=span), :]

    def line(j, p, t):
        return prod[j, p, pl.ds(start + t, 8, stride=span), :]

    def density(t, k):
        return load(src, K + k, t) - THERMAL / HALINE * load(src, k, t)

    def pressures(t):
        out = [density(t, 0)]
        for k in range(1, K):
            out.append(out[-1] + density(t, k))
        return out

    def fluxes(t):
        out = [None] * STATE
        for k in range(K):
            speed = None
            for f in (3, 0, 1, 2):
                p = f * K + k
                a = load(src, p, t) + load(src, p, t + 1)
                value = 7.0 * a - (load(src, p, t - 1) + load(src, p, t + 2))
                if f == 3:
                    speed = a
                out[p] = speed * value
        return out

    def row(t, carry):
        below_flux, p_prev, p_here = carry
        wet = coef(STATE + K, t) * mask
        wet24 = wet * (1.0 / 24.0)
        wet_grad = wet * (0.5 * GRAVITY * HALINE)
        wet_cor = wet * cor[pl.ds(start + t, 8, stride=span), :]
        p_next = pressures(t + 1)
        above = fluxes(t)
        grad_lon = None
        for k in range(K):
            wet_mix = wet * coef(STATE + k, t)
            drop = line(3, K + k, t) - THERMAL / HALINE * line(3, k, t)
            grad_lon = drop if k == 0 else grad_lon + drop
            u = load(src, 2 * K + k, t)
            mean = 6.0 * u + line(2, 2 * K + k, t)
            half = line(3, 2 * K + k, t)
            east_speed, west_speed = mean + half, mean - half
            for f in range(4):
                p = f * K + k
                q = load(src, p, t)
                adv = (east_speed * line(0, p, t) - west_speed * line(1, p, t)) + (above[p] - below_flux[p])
                lap = line(2, p, t) + (load(src, p, t + 1) + load(src, p, t - 1))
                if f < 2:
                    if 0 < k < K - 1:
                        lap = lap + (0.5 * (load(src, p - 1, t) + load(src, p + 1, t)) - q)
                    elif k == 0:
                        lap = lap + 0.5 * (load(src, p + 1, t) - q)
                    else:
                        lap = lap + 0.5 * (load(src, p - 1, t) - q)
                new = q + (wet_mix * lap - wet24 * adv)
                if f == 2:
                    new = new + (wet_cor * load(src, p + K, t) - wet_grad * grad_lon)
                if f == 3:
                    new = new - (wet_cor * load(src, p - K, t) + wet_grad * (p_next[k] - p_prev[k]))
                dst(p, pl.ds(dst_start + t, 8, stride=span), new)
        return above, p_here, p_next

    init = (fluxes(-1), pressures(-1), pressures(0))
    lax.fori_loop(0, span, row, init, unroll=unroll)


def window(tile, cor, seams, weights, prod, even, odd, out):
    span_rows = tile.shape[1] - 2 * PAD
    lane = lax.broadcasted_iota(jnp.int32, (8, LANES), 1)
    room = jnp.full((8, LANES), LANES, jnp.int32)
    for seam in seams:
        after = lax.rem(lane - seam + LANES, LANES)
        room = jnp.minimum(room, jnp.minimum(after, LANES - 1 - after))
    src = tile
    for s in range(STEPS):
        span = SPANS[s]
        need = span_rows - 4 * (s + 1)
        spare = (8 * span - need) // 2
        start = PAD + 2 * (s + 1) - spare
        keep = even if s % 2 == 0 else odd

        def put(p, rows, new, keep=keep):
            keep[p, rows, :] = new

        dst = out if s == STEPS - 1 else put
        dst_start = PAD - spare if s == STEPS - 1 else start
        lowest = PAD + 2 * (s + 1)
        first = lowest // 8 * 8
        count = -(-(lowest + need - first) // 16) * 16
        products(src, weights, prod, first, count)

        def coef(p, t, start=start, span=span):
            return tile[p, pl.ds(start + t, 8, stride=span), :]

        mask = jnp.where(room >= 2 * (s + 1), 1.0, 0.0)
        substep(src, dst, coef, cor, prod, mask, start, dst_start, span)
        src = keep


def interior_kernel(seam, tile, cor, weights, out, even, odd, prod):
    def put(p, rows, new):
        out[p, rows, :] = new

    window(tile, cor, (seam,), weights, prod, even, odd, put)


def interior(tile, cor, weights, seam):
    rows = tile.shape[1]
    block = rows - 2 * PAD - 2 * HALO
    vmem = pl.BlockSpec(memory_space=pltpu.VMEM)
    f32 = jnp.float32
    return pl.pallas_call(
        functools.partial(interior_kernel, seam),
        in_specs=[vmem] * 3,
        out_specs=vmem,
        out_shape=jax.ShapeDtypeStruct((STATE, block + 2 * PAD, LANES), f32),
        scratch_shapes=[
            pltpu.VMEM((STATE, rows, LANES), f32),
            pltpu.VMEM((STATE, rows, LANES), f32),
            pltpu.VMEM((4, STATE, rows, LANES), f32),
        ],
        compiler_params=params(),
        name="interior",
    )(tile, cor, weights)


def edge_kernel(start, cor, weights, got_low, got_high, inner0, inner1, result, tile, even, odd, prod, out_low, out_high, sems):
    span = got_low.shape[1]
    block = result.shape[1]

    @pl.loop(0, span // 8, unroll=4)
    def _(g):
        r = pl.multiple_of(g * 8, 8)
        lane = lax.broadcasted_iota(jnp.int32, (8, LANES), 1)
        for p in range(PLANES):
            q = p % 8
            mine = jnp.logical_and(lane >= 16 * q, lane < 16 * q + 16)
            both = jnp.where(mine, got_high[p // 8, pl.ds(r, 8)], got_low[p // 8, pl.ds(r, 8)])
            mid = start[p, pl.ds(PAD + r, 8)]
            tile[p, pl.ds(PAD + r, 8)] = jnp.where(lane < 32, shifted(both, -16 * q), mid)

    def put(p, rows, new):
        lane = lax.broadcasted_iota(jnp.int32, (8, LANES), 1)
        lo = inner0[p, rows, :]
        hi = inner1[p, rows, :]
        out_low[p, rows, :] = jnp.where(lane < 16, shifted(new, -32), jnp.where(lane < 112, lo, hi))
        out_high[p, rows, :] = jnp.where(lane < 80, hi, new)

    window(tile, cor, (16, 64), weights, prod, even, odd, put)
    copies = []
    for i, half in enumerate((out_low, out_high)):
        source = half.at[:, pl.ds(PAD, block), :]
        copies.append(pltpu.make_async_copy(source, result.at[:, :, pl.ds(i * LANES, LANES)], sems.at[i]))
    for copy in copies:
        copy.start()
    for copy in copies:
        copy.wait()


def edges(start, cor, weights, got_low, got_high, inner0, inner1):
    rows = start.shape[1]
    block = rows - 2 * PAD - 2 * HALO
    f32 = jnp.float32
    vmem = pl.BlockSpec(memory_space=pltpu.VMEM)
    return pl.pallas_call(
        edge_kernel,
        in_specs=[vmem] * 7,
        out_specs=pl.BlockSpec(memory_space=pltpu.HBM),
        out_shape=jax.ShapeDtypeStruct((STATE, block, 2 * LANES), f32),
        scratch_shapes=[
            pltpu.VMEM((PLANES, rows, LANES), f32),
            pltpu.VMEM((STATE, rows, LANES), f32),
            pltpu.VMEM((STATE, rows, LANES), f32),
            pltpu.VMEM((4, STATE, rows, LANES), f32),
            pltpu.VMEM((STATE, block + 2 * PAD, LANES), f32),
            pltpu.VMEM((STATE, block + 2 * PAD, LANES), f32),
            pltpu.SemaphoreType.DMA((2,)),
        ],
        compiler_params=params(),
        name="edges",
    )(start, cor, weights, got_low, got_high, inner0, inner1)


def body(ocean_state, mixing, land_sea):
    block, cols = land_sea.shape
    n_lon, n_lat = lax.axis_size("lon"), lax.axis_size("lat")
    axes = ("lon", "lat")

    def at(i, l):
        return (i % n_lon) * n_lat + l

    pairs_b = [(at(i, l), at(i, l ^ 1)) for i in range(n_lon) for l in range(n_lat)]
    pairs_a = []
    for i in range(n_lon):
        for l in range(1, n_lat - 1, 2):
            pairs_a += [(at(i, l), at(i, l + 1)), (at(i, l + 1), at(i, l))]
        pairs_a.append((at(i, n_lat - 1), at(n_lon - 1 - i, n_lat - 1)))
    east = [(i, (i + 1) % n_lon) for i in range(n_lon)]
    west = [((i + 1) % n_lon, i) for i in range(n_lon)]

    x = ocean_state.reshape(STATE, block, cols)
    x, mixing, land_sea = (pltpu.with_memory_space_constraint(v, pltpu.HBM) for v in (x, mixing, land_sea))
    to_a, to_b = pack_rows(x, mixing, land_sea)
    ra = lax.ppermute(to_a, axes, pairs_a)
    rb = lax.ppermute(to_b, axes, pairs_b)
    *parts, cor, weights = extend(x, mixing, land_sea)
    tile0, tile1, tile2, send_low, send_high = halo_rows(ra, rb, *parts)
    inner0 = interior(tile0, cor, weights, 0)
    send_low, send_high, inner0 = lax.optimization_barrier((send_low, send_high, inner0))
    got_low = lax.ppermute(send_high, "lon", east)
    got_high = lax.ppermute(send_low, "lon", west)
    inner1 = interior(tile1, cor, weights, 96)
    out = edges(tile2, cor, weights, got_low, got_high, inner0, inner1)
    return out.reshape(ocean_state.shape)


def solution(mesh):
    in_specs = (P(None, None, "lat", "lon"), P(None, "lat", "lon"), P("lat", "lon"))
    out_specs = P(None, None, "lat", "lon")
    return jax.shard_map(body, mesh=mesh, in_specs=in_specs, out_specs=out_specs, check_vma=False)
```
